256 devices in a mesh: rows: 64 (over z_lo, y, x, core), cols: 4 (over z_hi).
Axes of the slice: x: 4, y: 4, z: 8 (z_hi: 4, z_lo: 2; z = z_hi * 2 + z_lo), core: 2. Of those that a mesh axis runs over, the one named last changes fastest.
Arguments:
- design: bfloat16 [256, 1048576], P(None, 'rows'), may hold values from -0.28125 to 0.28125
- targets: bfloat16 [128, 1048576], P('cols', 'rows'), may hold values from -8 to 8
- flip_bits: int32 [2, 1048576], P(None, 'rows'), may hold values from 0 to 1
- listed: int32 [2, 32768], P(None, 'rows'), may hold values from 0 to 16383
- block_order: int32 [2, 64, 16], P(None, 'rows'), may hold values from 0 to 15, each once within a row
Outputs:
- solution: float32 [256, 128], P(None, 'cols')
- residual: float32 [128, 1048576], P('cols', 'rows')
The draws below stay inside these ranges and needn't reach their ends.
Inputs may be any that keep to these rules, and one draw needn't show every extreme that they name: A group's listed rows are its own rows, counted from its first row; repeats may occur. `block_order`: for each step and group the 16 entries are a permutation.
All inputs are finite; a program needn't handle non-finite values.
Results may differ from the reference program's by a relative error of at most 0.017.
Values sent between devices are 32-bit elements; how exact they have to be, the bound alone decides.
A program may use at most 64 MiB of HBM per device.

```python
import math
import jax
import jax.numpy as jnp
from jax import lax

P_SIZE = 256
K = 128
HB = 1024
SEL_DEV = 512
ITERS = 2
ROWS_DEV = 16384
ROWS = 1048576
NBLK = 16
LISTED = 32768
N_ROWS = 64


def design_values(key):
    value_key = jax.random.fold_in(key, 7001)
    order_key = jax.random.fold_in(key, 7004)
    column_key = jax.random.fold_in(key, 7005)
    group_total = ROWS // ROWS_DEV
    ranking = jax.random.permutation(order_key, P_SIZE).astype(jnp.float32)
    unknown_scale = jnp.power(10.0, -ranking / (P_SIZE - 1))
    group_index = (jnp.arange(ROWS, dtype=jnp.int32) // ROWS_DEV).astype(jnp.float32)
    group_scale = jnp.power(3.0, 0.5 * (group_index / max(group_total - 1, 1) - 1.0))
    values = jnp.clip(jax.random.normal(value_key, (P_SIZE, ROWS), jnp.float32), -4.5, 4.5)
    column_scale = jnp.power(10.0, -jax.random.uniform(column_key, (ROWS,), jnp.float32, 0.0, 0.75))
    scaled = values * unknown_scale[:, None] * (group_scale * column_scale)[None, :]
    return scaled / math.sqrt(P_SIZE)


def draw_design(key, part):
    return design_values(key).astype(jnp.bfloat16)


def draw_targets(key, part):
    matrix = design_values(key)
    truth_key = jax.random.fold_in(key, 7002)
    noise_key = jax.random.fold_in(key, 7003)
    true_map = 2.5 * jax.random.normal(truth_key, (P_SIZE, K), jnp.float32)
    noise_part = 0.1 * jax.random.normal(noise_key, (K, ROWS), jnp.float32)
    fitted = jnp.dot(true_map.T, matrix, precision=lax.Precision.HIGHEST)
    return jnp.clip(fitted + noise_part, -8.0, 8.0).astype(jnp.bfloat16)


def set_ends(drawn, stream_key, smallest, largest):
    extent = drawn.shape
    place = [jax.random.randint(jax.random.fold_in(stream_key, axis), (), 0, extent[axis]) for axis in range(len(extent))]
    drawn = drawn.at[tuple(place)].set(smallest)
    longest = extent.index(max(extent))
    place[longest] = (place[longest] + 1) % extent[longest]
    return drawn.at[tuple(place)].set(largest)


def setup_inputs(seed: int = 0) -> dict:
    keys = jax.random.split(jax.random.key(seed), 6)
    design = draw_design(jax.random.fold_in(keys[5], 71), 0)
    targets = draw_targets(jax.random.fold_in(keys[5], 71), 0)
    flip_bits = set_ends(jax.random.randint(keys[2], (ITERS, ROWS), 0, 2), jax.random.fold_in(keys[2], 1), 0, 1).astype(jnp.int32)
    listed = set_ends(jax.random.randint(keys[3], (ITERS, LISTED), 0, ROWS_DEV), jax.random.fold_in(keys[3], 1), 0, ROWS_DEV - 1).astype(jnp.int32)
    block_order = jax.vmap(lambda own: jax.random.permutation(own, NBLK))(jax.random.split(keys[4], ITERS * N_ROWS)).reshape((ITERS, N_ROWS, NBLK)).astype(jnp.int32)
    return dict(design=design, targets=targets, flip_bits=flip_bits, listed=listed, block_order=block_order)


def parity_table(length):
    indices = jnp.arange(length, dtype=jnp.int32)
    parity = jnp.zeros((length, length), jnp.int32)
    for bit_index in range(length.bit_length() - 1):
        parity = parity ^ indices[:, None] >> bit_index & 1 & (indices[None, :] >> bit_index & 1)
    return (1 - 2 * parity).astype(jnp.float32)

def sketch_of(design_full, flips, listed_now, order_now, hadamard):
    sign_row = (2 * flips - 1).astype(jnp.float32)
    width_block = math.gcd(SEL_DEV, 128)
    inv_root = 1.0 / math.sqrt(HB)
    keep_scale = math.sqrt(ROWS_DEV / SEL_DEV)

    def one_group(running, group):
        start = (group * ROWS_DEV).astype(jnp.int32)
        local_rows = lax.dynamic_slice_in_dim(design_full, start, ROWS_DEV, 1)
        local_sign = lax.dynamic_slice_in_dim(sign_row, start, ROWS_DEV, 0)
        blocks = (local_rows * local_sign[None, :]).reshape(P_SIZE, NBLK, HB)
        chosen = lax.dynamic_slice_in_dim(listed_now, (group * SEL_DEV).astype(jnp.int32), SEL_DEV, 0)
        order_group = lax.dynamic_index_in_dim(order_now, group, 0, keepdims=False)
        source = jnp.take(order_group, chosen // HB)
        within = chosen % HB

        def columns(pair):
            src_block, spot = pair
            gathered = jnp.take(blocks, src_block, axis=1)
            picked = jnp.take(hadamard, spot, axis=1)
            return jnp.einsum('psh,hs->ps', gathered, picked, precision=lax.Precision.HIGHEST)
        values = lax.map(columns, (source.reshape(-1, width_block), within.reshape(-1, width_block)))
        values = jnp.moveaxis(values, 0, 1).reshape(P_SIZE, SEL_DEV)
        mixed_rows = (values * inv_root).astype(jnp.bfloat16)
        return (running + mixed_rows.astype(jnp.float32) * keep_scale, None)
    start_sum = jnp.zeros((P_SIZE, SEL_DEV), jnp.float32)
    total, _ = lax.scan(one_group, start_sum, jnp.arange(N_ROWS, dtype=jnp.int32))
    return total

def reference(design, targets, flip_bits, listed, block_order):
    design_full = design.astype(jnp.float32)
    target_full = targets.astype(jnp.float32)
    hadamard = parity_table(HB)
    solution = jnp.zeros((P_SIZE, K), jnp.float32)
    for step_index in range(ITERS):
        sketch = sketch_of(design_full, flip_bits[step_index], listed[step_index], block_order[step_index], hadamard)
        sketch_gram = jnp.dot(sketch, sketch.T, precision=lax.Precision.HIGHEST)
        gram_now = sketch_gram + jnp.trace(sketch_gram) / P_SIZE * jnp.eye(P_SIZE, dtype=jnp.float32)
        half_iterate = solution.astype(jnp.bfloat16).astype(jnp.float32)
        misfit = jnp.dot(half_iterate.T, design_full, precision=lax.Precision.HIGHEST) - target_full
        misfit_half = misfit.astype(jnp.bfloat16).astype(jnp.float32)
        gradient = jnp.dot(design_full, misfit_half.T, precision=lax.Precision.HIGHEST)
        factor = jnp.linalg.cholesky(gram_now)
        solution = solution - jax.scipy.linalg.cho_solve((factor, True), gradient)
    half_iterate = solution.astype(jnp.bfloat16).astype(jnp.float32)
    residual = jnp.dot(half_iterate.T, design_full, precision=lax.Precision.HIGHEST) - target_full
    return (solution, residual)
```

```python
import functools
import math

import jax
import jax.numpy as jnp
from jax import lax
from jax.experimental import pallas as pl
from jax.experimental.pallas import tpu as pltpu
from jax.sharding import PartitionSpec as P

MESH = pl.DeviceIdType.MESH
F32 = jnp.float32
BF16 = jnp.bfloat16
NB = 32
NT = (((1,), (1,)), ((), ()))
TN = (((0,), (0,)), ((), ()))
HIGHEST = lax.Precision.HIGHEST


def split(x):
    hi = x.astype(BF16)
    return hi, (x - hi.astype(F32)).astype(BF16)


def kernel(
    order_ref,
    design_ref,
    targets_ref,
    flips_ref,
    listed_ref,
    out_ref,
    dv,
    tv,
    fv,
    lv,
    walsh,
    srcs,
    lhs_a,
    lhs_b,
    acc,
    xs,
    xe,
    rs_s,
    rs_e,
    sf,
    ef,
    mat,
    gmat,
    bt,
    xsend,
    xrecv,
    ysend,
    yrecv,
    in_sems,
    send_sems,
    recv_sems,
):
    unknowns = dv.shape[0]
    rows_here = dv.shape[1]
    block_len = walsh.shape[1]
    blocks = rows_here // block_len
    steps = 2
    picks = 128
    inv_root = 1.0 / math.sqrt(block_len)
    keep_scale = math.sqrt(rows_here / listed_ref.shape[1])
    row = lax.axis_index("rows")
    col = lax.axis_index("cols")
    core = row % 2
    xy = (row // 2) % 16
    z_lo = row // 32
    z = col * 2 + z_lo

    def chunk_copy(b):
        lanes = pl.ds(b * block_len, block_len)
        return pltpu.make_async_copy(design_ref.at[:, lanes], dv.at[:, lanes], in_sems.at[b])

    small = (
        pltpu.make_async_copy(listed_ref, lv, in_sems.at[blocks]),
        pltpu.make_async_copy(flips_ref, fv, in_sems.at[blocks + 1]),
        pltpu.make_async_copy(targets_ref, tv, in_sems.at[blocks + 2]),
    )
    small[0].start()
    small[1].start()
    chunk_copy(0).start()
    small[2].start()
    for b in range(1, blocks):
        chunk_copy(b).start()

    barrier = pltpu.get_barrier_semaphore()

    @pl.loop(1, 64)
    def _(k):
        pl.semaphore_signal(
            barrier, inc=1, device_id=((row + k) % 64, col), device_id_type=MESH
        )

    def z_peer(k):
        other = (z + k) % 8
        return ((other % 2) * 32 + row % 32, other // 2)

    for k in range(1, 8):

        @pl.when(((z + k) % 8) // 2 != col)
        def _():
            pl.semaphore_signal(barrier, inc=1, device_id=z_peer(k), device_id_type=MESH)

    small[0].wait()
    picked = lv[:, pl.ds(pl.multiple_of(col * picks, picks), picks)]
    eye = lax.broadcasted_iota(jnp.int32, (picks, picks), 0) == lax.broadcasted_iota(
        jnp.int32, (picks, picks), 1
    )
    for t in range(steps):
        line = picked[t : t + 1, :]
        target_block = line // block_len
        source = jnp.zeros_like(line)
        for b in range(blocks):
            source = jnp.where(target_block == b, order_ref[t, b], source)
        code = (source * block_len + line % block_len).astype(F32)
        column = jnp.sum(
            jnp.where(eye, jnp.broadcast_to(code, (picks, picks)), 0.0), axis=1, keepdims=True
        ).astype(jnp.int32)
        srcs[t * picks : (t + 1) * picks, :] = jnp.broadcast_to(column // block_len, (picks, 128))
        within = column % block_len
        for h in range(block_len // 128):
            places = lax.broadcasted_iota(jnp.int32, (picks, 128), 1) + h * 128
            bits = within & places
            bits = bits ^ (bits >> 8)
            bits = bits ^ (bits >> 4)
            bits = bits ^ (bits >> 2)
            bits = (bits ^ (bits >> 1)) & 1
            walsh[t * picks : (t + 1) * picks, h * 128 : (h + 1) * 128] = (
                (1 - 2 * bits).astype(F32).astype(BF16)
            )
    small[1].wait()
    small[2].wait()
    acc[...] = jnp.zeros_like(acc)

    def block_terms(b, lhs):
        lanes = pl.ds(pl.multiple_of(b * block_len, block_len), block_len)
        pltpu.make_async_copy(
            design_ref.at[:, lanes], dv.at[:, lanes], in_sems.at[b]
        ).wait()
        for t in range(steps):
            own = slice(t * picks, (t + 1) * picks)
            sign = (2 * fv[t : t + 1, lanes] - 1).astype(F32).astype(BF16)
            chosen = jnp.where(srcs[own, 0:128] == b, 1.0, 0.0).astype(BF16)
            for h in range(block_len // 128):
                part = slice(h * 128, (h + 1) * 128)
                lhs[own, part] = walsh[own, part] * chosen * sign[:, part]
        first = steps * picks
        lhs[first : first + 64, :] = dv[pl.ds(pl.multiple_of(col * 64, 64), 64), lanes]
        lhs[first + 64 : first + 96, :] = tv[:, lanes]
        acc[...] += lax.dot_general(lhs[...], dv[:, lanes], NT, preferred_element_type=F32)

    @pl.loop(0, blocks // 2)
    def _(pair):
        block_terms(2 * pair, lhs_a)
        block_terms(2 * pair + 1, lhs_b)

    for half in range(2):
        lanes = slice(half * 128, (half + 1) * 128)
        for rb in range(16):
            for t in range(steps):
                first = t * picks + rb * 8
                tile = (acc[first : first + 8, lanes] * inv_root).astype(BF16)
                xs[2 * (half * 16 + rb) + t] = tile.astype(F32) * keep_scale
            first = 2 * picks + rb * 4
            xe[2 * (half * 16 + rb) + 1] = acc[first : first + 4, lanes]
            if rb < 8:
                first = 2 * picks + 64 + rb * 4
                xe[2 * (half * 16 + rb)] = acc[first : first + 4, lanes]
            else:
                xe[2 * (half * 16 + rb)] = jnp.zeros((4, 128), F32)

    pl.semaphore_wait(barrier, 63 + 6)

    def remote(src, dst, stage, peer):
        return pltpu.make_async_remote_copy(
            src_ref=src,
            dst_ref=dst,
            send_sem=send_sems.at[stage],
            recv_sem=recv_sems.at[stage],
            device_id=peer,
            device_id_type=MESH,
        )

    def scatter(src, dst, stage):
        @pl.loop(1, 64)
        def _(k):
            peer = (row + k) % 64
            remote(src.at[peer], dst.at[k - 1], stage, (peer, col)).start()

    def gather_z(full, stage):
        @pl.loop(1, 8)
        def _(k):
            place = full.at[z, xy]
            remote(place, place, stage, z_peer(k)).start()

    def gather_xy(full, stage):
        @pl.loop(1, 16)
        def _(k):
            place = full.at[:, xy]
            peer = z_lo * 32 + ((xy + k) % 16) * 2 + core
            remote(place, place, stage, (peer, col)).start()

    def all_of(buffer, stage):
        return remote(buffer, buffer, stage, (row, col))

    def total(own, parts):
        sums = [own]
        for lead in range(3):
            sums.append(parts[lead])
        for index in range(3, 63):
            sums[index % 4] = sums[index % 4] + parts[index]
        return (sums[0] + sums[1]) + (sums[2] + sums[3])

    scatter(xs, rs_s, 0)
    scatter(xe, rs_e, 1)
    all_of(rs_s, 0).wait_recv()
    sf[z, xy] = total(xs[row], rs_s)
    gather_z(sf, 2)
    all_of(rs_e, 1).wait_recv()
    ef[z, xy] = total(xe[row], rs_e)
    gather_z(ef, 3)
    all_of(rs_s.at[0:7], 2).wait_recv()
    gather_xy(sf, 4)
    all_of(rs_e.at[0:7], 3).wait_recv()
    gather_xy(ef, 5)
    all_of(sf.at[:, 0:15], 4).wait_recv()

    squares = jnp.zeros((8, 128), F32)
    halves = []
    for half in range(2):
        parts = [sf[2 * c + half].reshape(picks, 128) for c in range(4)]
        halves.append(jnp.concatenate(parts, axis=0))
    sketch = jnp.concatenate(halves, axis=1)
    for first in range(0, 512, 8):
        for lane in range(0, 256, 128):
            piece = sketch[first : first + 8, lane : lane + 128]
            squares = squares + piece * piece
    hi, lo = split(sketch)
    gram = lax.dot_general(hi, hi, TN, preferred_element_type=F32)
    gram = gram + lax.dot_general(hi, lo, TN, preferred_element_type=F32)
    gram = gram + lax.dot_general(lo, hi, TN, preferred_element_type=F32)
    shift = jnp.sum(squares) / unknowns
    diagonal = lax.broadcasted_iota(jnp.int32, (unknowns, unknowns), 0) == lax.broadcasted_iota(
        jnp.int32, (unknowns, unknowns), 1
    )
    mat[...] = gram + jnp.where(diagonal, shift, 0.0)

    lane_ids = lax.broadcasted_iota(jnp.int32, (NB, unknowns), 1)
    row_ids = lax.broadcasted_iota(jnp.int32, (NB, unknowns), 0)
    for k0 in range(0, unknowns, NB):
        band = slice(k0, k0 + NB)
        panel = mat[band, :]
        signed = jnp.where(lane_ids < k0, -panel, panel)
        left_hi, left_lo = split(signed)
        left = jnp.concatenate([left_hi, left_hi, left_lo], axis=0)
        for j in range(NB):
            c = k0 + j
            column = panel[:, c : c + 1]
            inverse = 1.0 / panel[j : j + 1, c : c + 1]
            cleared = jnp.where(lane_ids == c, 0.0, panel)
            line = jnp.where(lane_ids[0:1] == c, 1.0, panel[j : j + 1, :]) * inverse
            panel = jnp.where(row_ids == j, line, cleared - column * line)
        right_hi, right_lo = split(panel)
        right = jnp.concatenate([right_hi, right_lo, right_hi], axis=0)
        update = lax.dot_general(left, right, TN, preferred_element_type=F32)
        for other in range(0, unknowns, NB):
            here = slice(other, other + NB)
            if other == k0:
                mat[here, :] = panel
            else:
                kept = jnp.where((lane_ids >= k0) & (lane_ids < k0 + NB), 0.0, mat[here, :])
                mat[here, :] = kept - update[here, :]

    all_of(ef.at[:, 0:15], 5).wait_recv()

    @pl.when(core == 0)
    def _():
        for half in range(2):
            for rb in range(8):
                bt[rb * 4 : rb * 4 + 4, half * 128 : (half + 1) * 128] = ef[2 * col + half, rb]
        first = jnp.dot(bt[...], mat[...], precision=HIGHEST, preferred_element_type=F32)
        xsend[0:32, :] = first
        xsend[32:64, :] = bt[...]
        handed = remote(xsend, xrecv, 6, (row + 1, col))
        handed.start()
        remote(ysend, yrecv, 7, (row + 1, col)).wait_recv()
        out_ref[...] = yrecv[...]
        handed.wait_send()

    @pl.when(core == 1)
    def _():
        for c in range(4):
            for half in range(2):
                for rb in range(16):
                    first = c * 64 + rb * 4
                    gmat[first : first + 4, half * 128 : (half + 1) * 128] = ef[2 * c + half, rb]
        remote(xsend, xrecv, 6, (row - 1, col)).wait_recv()
        start = xrecv[0:32, :]
        rounded = start.astype(BF16).astype(F32)
        gradient = jnp.dot(rounded, gmat[...], precision=HIGHEST, preferred_element_type=F32)
        gradient = gradient - xrecv[32:64, :]
        moved = start - jnp.dot(gradient, mat[...], precision=HIGHEST, preferred_element_type=F32)
        ysend[...] = moved
        handed = remote(ysend, yrecv, 7, (row - 1, col))
        handed.start()
        out_ref[...] = moved
        handed.wait_send()

    all_of(rs_s, 0).wait_send()
    all_of(rs_e, 1).wait_send()
    all_of(rs_s.at[0:7], 2).wait_send()
    all_of(rs_e.at[0:7], 3).wait_send()
    all_of(sf.at[:, 0:15], 4).wait_send()
    all_of(ef.at[:, 0:15], 5).wait_send()


def on_device(design, targets, flip_bits, listed, block_order):
    unknowns, rows_here = design.shape
    block_len = rows_here // block_order.shape[2]
    rhs = targets.shape[0]
    any_space = pl.BlockSpec(memory_space=pl.ANY)
    solved = pl.pallas_call(
        kernel,
        out_shape=jax.ShapeDtypeStruct((rhs, unknowns), F32),
        in_specs=[pl.BlockSpec(memory_space=pltpu.SMEM)] + [any_space] * 4,
        out_specs=pl.BlockSpec(memory_space=pltpu.VMEM),
        scratch_shapes=[
            pltpu.VMEM((unknowns, rows_here), BF16),
            pltpu.VMEM((rhs, rows_here), BF16),
            pltpu.VMEM((2, rows_here), jnp.int32),
            pltpu.VMEM((2, 512), jnp.int32),
            pltpu.VMEM((256, block_len), BF16),
            pltpu.VMEM((256, 128), jnp.int32),
            pltpu.VMEM((352, block_len), BF16),
            pltpu.VMEM((352, block_len), BF16),
            pltpu.VMEM((352, unknowns), F32),
            pltpu.VMEM((64, 8, 128), F32),
            pltpu.VMEM((64, 4, 128), F32),
            pltpu.VMEM((63, 8, 128), F32),
            pltpu.VMEM((63, 4, 128), F32),
            pltpu.VMEM((8, 16, 8, 128), F32),
            pltpu.VMEM((8, 16, 4, 128), F32),
            pltpu.VMEM((unknowns, unknowns), F32),
            pltpu.VMEM((unknowns, unknowns), F32),
            pltpu.VMEM((rhs, unknowns), F32),
            pltpu.VMEM((2 * rhs, unknowns), F32),
            pltpu.VMEM((2 * rhs, unknowns), F32),
            pltpu.VMEM((rhs, unknowns), F32),
            pltpu.VMEM((rhs, unknowns), F32),
            pltpu.SemaphoreType.DMA((block_order.shape[2] + 3,)),
            pltpu.SemaphoreType.DMA((8,)),
            pltpu.SemaphoreType.DMA((8,)),
        ],
        compiler_params=pltpu.CompilerParams(
            collective_id=0, has_side_effects=True, vmem_limit_bytes=40 * 1024 * 1024
        ),
        name="sketch_solve",
    )(block_order.reshape(2, block_order.shape[2]), design, targets, flip_bits, listed)
    residual = jnp.dot(
        solved.astype(BF16), design, preferred_element_type=F32
    ) - targets.astype(F32)
    return (solved.T, residual)


def solution(mesh):
    return jax.shard_map(
        on_device,
        mesh=mesh,
        in_specs=(
            P(None, "rows"),
            P("cols", "rows"),
            P(None, "rows"),
            P(None, "rows"),
            P(None, "rows", None),
        ),
        out_specs=(P(None, "cols"), P("cols", "rows")),
        check_vma=False,
    )
```

```python
import functools
import math

import jax
import jax.numpy as jnp
from jax import lax
from jax.experimental import pallas as pl
from jax.experimental.pallas import tpu as pltpu
from jax.sharding import PartitionSpec as P

MESH = pl.DeviceIdType.MESH
F32 = jnp.float32
BF16 = jnp.bfloat16
NB = 32
NT = (((1,), (1,)), ((), ()))
TN = (((0,), (0,)), ((), ()))
HIGHEST = lax.Precision.HIGHEST


def split(x):
    hi = x.astype(BF16)
    return hi, (x - hi.astype(F32)).astype(BF16)


def lane_of(tile, c):
    return jnp.broadcast_to(tile[:, c : c + 1], (8, 128))


def row_of(tile, j):
    return jnp.broadcast_to(tile[j : j + 1, :], (8, 128))


def tree(terms):
    while len(terms) > 1:
        paired = [terms[i] + terms[i + 1] for i in range(0, len(terms) - 1, 2)]
        terms = paired + ([terms[-1]] if len(terms) % 2 else [])
    return terms[0]


def small_inverse(cols, sub):
    for q in range(0, 8, 2):
        a, b, c = row_of(cols[q], q), row_of(cols[q + 1], q), row_of(cols[q + 1], q + 1)
        r = 1.0 / (a * c - b * b)
        p00, p01, p11 = c * r, -b * r, a * r
        w0 = -(cols[q] * p00 + cols[q + 1] * p01)
        w1 = -(cols[q] * p01 + cols[q + 1] * p11)
        w0 = jnp.where(sub == q, p00, jnp.where(sub == q + 1, p01, w0))
        w1 = jnp.where(sub == q, p01, jnp.where(sub == q + 1, p11, w1))
        fresh = []
        for j in range(8):
            if j == q:
                fresh.append(w0)
            elif j == q + 1:
                fresh.append(w1)
            else:
                kept = jnp.where((sub == q) | (sub == q + 1), 0.0, cols[j])
                fresh.append(kept + (w0 * row_of(cols[j], q) + w1 * row_of(cols[j], q + 1)))
        cols = fresh
    return cols


def eliminate(tiles, k0, sub, lane):
    home = k0 // 128
    groups = NB // 8
    for s in range(groups):
        c0 = k0 + 8 * s - 128 * home
        cols = [[lane_of(tiles[g][home], c0 + j) for g in range(groups)] for j in range(8)]
        inverse = small_inverse([cols[j][s] for j in range(8)], sub)
        inside = (lane >= c0) & (lane < c0 + 8)
        unit = jnp.where(lane == sub + c0, 1.0, 0.0)
        lead = [jnp.where(inside, unit, t) if h == home else t for h, t in enumerate(tiles[s])]
        fresh = [tree([inverse[j] * row_of(lead[h], j) for j in range(8)]) for h in range(2)]
        rows = [[row_of(fresh[h], j) for j in range(8)] for h in range(2)]
        after = []
        for g in range(groups):
            if g == s:
                after.append(fresh)
                continue
            line = []
            for h in range(2):
                kept = jnp.where(inside, 0.0, tiles[g][h]) if h == home else tiles[g][h]
                line.append(kept - tree([cols[j][g] * rows[h][j] for j in range(8)]))
            after.append(line)
        tiles = after
    return tiles


def invert(mat):
    n = mat.shape[0]
    sub = lax.broadcasted_iota(jnp.int32, (8, 128), 0)
    lane = lax.broadcasted_iota(jnp.int32, (8, 128), 1)
    wide = lax.broadcasted_iota(jnp.int32, (NB, n), 1)
    panel = mat[0:NB, :]
    for k0 in range(0, n, NB):
        k1 = k0 + NB
        left_hi, left_lo = split(jnp.where(wide < k0, -panel, panel))
        left = jnp.concatenate([left_hi, left_hi, left_lo], axis=0)
        tiles = [
            [panel[8 * g : 8 * g + 8, 128 * h : 128 * h + 128] for h in range(2)]
            for g in range(NB // 8)
        ]
        tiles = eliminate(tiles, k0, sub, lane)
        done = jnp.concatenate([jnp.concatenate(t, axis=1) for t in tiles], axis=0)
        right_hi, right_lo = split(done)
        right = jnp.concatenate([right_hi, right_lo, right_hi], axis=0)
        inside = (wide >= k0) & (wide < k1)
        if k1 < n:
            first = lax.dot_general(left[:, k1 : k1 + NB], right, TN, preferred_element_type=F32)
            panel = jnp.where(inside, 0.0, mat[k1 : k1 + NB, :]) - first
        update = lax.dot_general(left, right, TN, preferred_element_type=F32)
        for other in range(0, n, NB):
            here = slice(other, other + NB)
            if other == k0:
                mat[here, :] = done
            elif other != k1:
                mat[here, :] = jnp.where(inside, 0.0, mat[here, :]) - update[here, :]


def kernel(
    order_ref,
    design_ref,
    targets_ref,
    flips_ref,
    listed_ref,
    out_ref,
    dv,
    tv,
    order,
    fv,
    lv,
    walsh,
    srcs,
    lhs,
    acc,
    acc_e,
    xs,
    xe,
    rs_s,
    rs_e,
    sf,
    ef,
    mat,
    gmat,
    bt,
    xsend,
    xrecv,
    ysend,
    yrecv,
    in_sems,
    send_sems,
    recv_sems,
):
    unknowns = dv.shape[0]
    rows_here = dv.shape[1]
    block_len = walsh.shape[1]
    blocks = rows_here // block_len
    steps = 2
    picks = 128
    inv_root = 1.0 / math.sqrt(block_len)
    keep_scale = math.sqrt(rows_here / listed_ref.shape[1])
    row = lax.axis_index("rows")
    col = lax.axis_index("cols")
    core = row % 2
    xy = (row // 2) % 16
    z_lo = row // 32
    z = col * 2 + z_lo

    def chunk_copy(b):
        lanes = pl.ds(b * block_len, block_len)
        return pltpu.make_async_copy(design_ref.at[:, lanes], dv.at[:, lanes], in_sems.at[b])

    small = (
        pltpu.make_async_copy(order_ref, order, in_sems.at[blocks + 3]),
        pltpu.make_async_copy(listed_ref, lv, in_sems.at[blocks]),
        pltpu.make_async_copy(flips_ref, fv, in_sems.at[blocks + 1]),
        pltpu.make_async_copy(targets_ref, tv, in_sems.at[blocks + 2]),
    )
    small[0].start()
    small[1].start()
    small[2].start()
    chunk_copy(0).start()
    small[3].start()
    for b in range(1, blocks):
        chunk_copy(b).start()

    barrier = pltpu.get_barrier_semaphore()

    def z_peer(k):
        other = (z + k) % 8
        return ((other % 2) * 32 + row % 32, other // 2)

    for k in range(1, 8):

        @pl.when(((z + k) % 8) // 2 != col)
        def _():
            pl.semaphore_signal(barrier, inc=1, device_id=z_peer(k), device_id_type=MESH)

    small[0].wait()
    small[1].wait()
    picked = lv[:, pl.ds(pl.multiple_of(col * picks, picks), picks)]
    eye = lax.broadcasted_iota(jnp.int32, (picks, picks), 0) == lax.broadcasted_iota(
        jnp.int32, (picks, picks), 1
    )
    for t in range(steps):
        line = picked[t : t + 1, :]
        target_block = line // block_len
        source = jnp.zeros_like(line)
        for b in range(blocks):
            source = jnp.where(target_block == b, order[t, b], source)
        code = (source * block_len + line % block_len).astype(F32)
        column = jnp.sum(
            jnp.where(eye, jnp.broadcast_to(code, (picks, picks)), 0.0), axis=1, keepdims=True
        ).astype(jnp.int32)
        srcs[t * picks : (t + 1) * picks, :] = jnp.broadcast_to(column // block_len, (picks, 128))
        within = column % block_len
        for h in range(block_len // 128):
            places = lax.broadcasted_iota(jnp.int32, (picks, 128), 1) + h * 128
            bits = within & places
            bits = bits ^ (bits >> 8)
            bits = bits ^ (bits >> 4)
            bits = bits ^ (bits >> 2)
            bits = (bits ^ (bits >> 1)) & 1
            walsh[t * picks : (t + 1) * picks, h * 128 : (h + 1) * 128] = (
                (1 - 2 * bits).astype(F32).astype(BF16)
            )
    small[2].wait()
    width = 2 * block_len
    acc[...] = jnp.zeros_like(acc)

    @pl.loop(0, blocks // 2)
    def _(pair):
        @pl.when(pair < 7)
        def _():
            for k in range(9):
                peer = (row + pair * 9 + k + 1) % 64
                pl.semaphore_signal(barrier, inc=1, device_id=(peer, col), device_id_type=MESH)

        lanes = pl.ds(pl.multiple_of(pair * width, width), width)
        for b in range(2):
            here = pl.ds(pl.multiple_of(pair * width, width) + b * block_len, block_len)
            pltpu.make_async_copy(
                design_ref.at[:, here], dv.at[:, here], in_sems.at[2 * pair + b]
            ).wait()
            for t in range(steps):
                own = slice(t * picks, (t + 1) * picks)
                sign = (2 * fv[t : t + 1, here] - 1).astype(F32).astype(BF16)
                chosen = jnp.where(srcs[own, :] == 2 * pair + b, 1.0, 0.0).astype(BF16)
                for h in range(block_len // 128):
                    part = slice(h * 128, (h + 1) * 128)
                    place = slice(b * block_len + h * 128, b * block_len + (h + 1) * 128)
                    lhs[own, place] = walsh[own, part] * chosen * sign[:, part]
        acc[...] += lax.dot_general(lhs[...], dv[:, lanes], NT, preferred_element_type=F32)

    for half in range(2):
        lanes = slice(half * 128, (half + 1) * 128)
        for rb in range(16):
            for t in range(steps):
                first = t * picks + rb * 8
                tile = (acc[first : first + 8, lanes] * inv_root).astype(BF16)
                xs[2 * (half * 16 + rb) + t] = tile.astype(F32) * keep_scale

    pl.semaphore_wait(barrier, 63 + 6)

    def remote(src, dst, stage, peer):
        return pltpu.make_async_remote_copy(
            src_ref=src,
            dst_ref=dst,
            send_sem=send_sems.at[stage],
            recv_sem=recv_sems.at[stage],
            device_id=peer,
            device_id_type=MESH,
        )

    def scatter(src, dst, stage):
        @pl.loop(1, 64)
        def _(k):
            peer = (row + k) % 64
            remote(src.at[peer], dst.at[k - 1], stage, (peer, col)).start()

    def gather_z(full, stage):
        @pl.loop(1, 8)
        def _(k):
            place = full.at[z, xy]
            remote(place, place, stage, z_peer(k)).start()

    def gather_xy(full, stage):
        @pl.loop(1, 16)
        def _(k):
            place = full.at[:, xy]
            peer = z_lo * 32 + ((xy + k) % 16) * 2 + core
            remote(place, place, stage, (peer, col)).start()

    def all_of(buffer, stage):
        return remote(buffer, buffer, stage, (row, col))

    def total(own, parts):
        sums = [own]
        for lead in range(3):
            sums.append(parts[lead])
        for index in range(3, 63):
            sums[index % 4] = sums[index % 4] + parts[index]
        return (sums[0] + sums[1]) + (sums[2] + sums[3])

    scatter(xs, rs_s, 0)

    small[3].wait()
    acc_e[...] = jnp.zeros_like(acc_e)

    @pl.loop(0, blocks // 4)
    def _(part):
        lanes = pl.ds(pl.multiple_of(part * 2 * width, 2 * width), 2 * width)
        own = dv[pl.ds(pl.multiple_of(col * 64, 64), 64), lanes]
        both = jnp.concatenate([own, tv[:, lanes]], axis=0)
        acc_e[...] += lax.dot_general(both, dv[:, lanes], NT, preferred_element_type=F32)

    for half in range(2):
        lanes = slice(half * 128, (half + 1) * 128)
        for rb in range(16):
            xe[2 * (half * 16 + rb) + 1] = acc_e[rb * 4 : rb * 4 + 4, lanes]
            if rb < 8:
                xe[2 * (half * 16 + rb)] = acc_e[64 + rb * 4 : 68 + rb * 4, lanes]
            else:
                xe[2 * (half * 16 + rb)] = jnp.zeros((4, 128), F32)
    scatter(xe, rs_e, 1)
    all_of(rs_s, 0).wait_recv()
    sf[z, xy] = total(xs[row], rs_s)
    gather_z(sf, 2)
    all_of(rs_e, 1).wait_recv()
    ef[z, xy] = total(xe[row], rs_e)
    gather_z(ef, 3)
    all_of(rs_s.at[0:7], 2).wait_recv()
    gather_xy(sf, 4)
    all_of(rs_e.at[0:7], 3).wait_recv()
    gather_xy(ef, 5)
    all_of(sf.at[:, 0:15], 4).wait_recv()

    squares = jnp.zeros((8, 128), F32)
    halves = []
    for half in range(2):
        parts = [sf[2 * c + half].reshape(picks, 128) for c in range(4)]
        halves.append(jnp.concatenate(parts, axis=0))
    sketch = jnp.concatenate(halves, axis=1)
    for first in range(0, 512, 8):
        for lane in range(0, 256, 128):
            piece = sketch[first : first + 8, lane : lane + 128]
            squares = squares + piece * piece
    hi, lo = split(sketch)
    gram = lax.dot_general(hi, hi, TN, preferred_element_type=F32)
    gram = gram + lax.dot_general(hi, lo, TN, preferred_element_type=F32)
    gram = gram + lax.dot_general(lo, hi, TN, preferred_element_type=F32)
    shift = jnp.sum(squares) / unknowns
    diagonal = lax.broadcasted_iota(jnp.int32, (unknowns, unknowns), 0) == lax.broadcasted_iota(
        jnp.int32, (unknowns, unknowns), 1
    )
    mat[...] = gram + jnp.where(diagonal, shift, 0.0)

    invert(mat)

    all_of(ef.at[:, 0:15], 5).wait_recv()

    @pl.when(core == 0)
    def _():
        for half in range(2):
            for rb in range(8):
                bt[rb * 4 : rb * 4 + 4, half * 128 : (half + 1) * 128] = ef[2 * col + half, rb]
        first = jnp.dot(bt[...], mat[...], precision=HIGHEST, preferred_element_type=F32)
        xsend[0:32, :] = first
        xsend[32:64, :] = bt[...]
        handed = remote(xsend, xrecv, 6, (row + 1, col))
        handed.start()
        remote(ysend, yrecv, 7, (row + 1, col)).wait_recv()
        out_ref[...] = yrecv[...]
        handed.wait_send()

    @pl.when(core == 1)
    def _():
        for c in range(4):
            for half in range(2):
                for rb in range(16):
                    first = c * 64 + rb * 4
                    gmat[first : first + 4, half * 128 : (half + 1) * 128] = ef[2 * c + half, rb]
        remote(xsend, xrecv, 6, (row - 1, col)).wait_recv()
        start = xrecv[0:32, :]
        rounded = start.astype(BF16).astype(F32)
        gradient = jnp.dot(rounded, gmat[...], precision=HIGHEST, preferred_element_type=F32)
        gradient = gradient - xrecv[32:64, :]
        moved = start - jnp.dot(gradient, mat[...], precision=HIGHEST, preferred_element_type=F32)
        ysend[...] = moved
        handed = remote(ysend, yrecv, 7, (row - 1, col))
        handed.start()
        out_ref[...] = moved
        handed.wait_send()

    all_of(rs_s, 0).wait_send()
    all_of(rs_e, 1).wait_send()
    all_of(rs_s.at[0:7], 2).wait_send()
    all_of(rs_e.at[0:7], 3).wait_send()
    all_of(sf.at[:, 0:15], 4).wait_send()
    all_of(ef.at[:, 0:15], 5).wait_send()


def on_device(design, targets, flip_bits, listed, block_order):
    unknowns, rows_here = design.shape
    block_len = rows_here // block_order.shape[2]
    rhs = targets.shape[0]
    order = block_order.reshape(2, block_order.shape[2])
    given = (order, design, targets, flip_bits, listed)
    solved, near_design, near_targets = pl.pallas_call(
        kernel,
        out_shape=(
            jax.ShapeDtypeStruct((rhs, unknowns), F32),
            jax.ShapeDtypeStruct(design.shape, BF16),
            jax.ShapeDtypeStruct(targets.shape, BF16),
        ),
        in_specs=[pl.BlockSpec(memory_space=pltpu.HBM)] * 5,
        out_specs=[pl.BlockSpec(memory_space=pltpu.VMEM)] * 3,
        scratch_shapes=[
            pltpu.SMEM((2, block_order.shape[2]), jnp.int32),
            pltpu.VMEM((2, rows_here), jnp.int32),
            pltpu.VMEM((2, 512), jnp.int32),
            pltpu.VMEM((256, block_len), BF16),
            pltpu.VMEM((256, 128), jnp.int32),
            pltpu.VMEM((256, 2 * block_len), BF16),
            pltpu.VMEM((256, unknowns), F32),
            pltpu.VMEM((96, unknowns), F32),
            pltpu.VMEM((64, 8, 128), F32),
            pltpu.VMEM((64, 4, 128), F32),
            pltpu.VMEM((63, 8, 128), F32),
            pltpu.VMEM((63, 4, 128), F32),
            pltpu.VMEM((8, 16, 8, 128), F32),
            pltpu.VMEM((8, 16, 4, 128), F32),
            pltpu.VMEM((unknowns, unknowns), F32),
            pltpu.VMEM((unknowns, unknowns), F32),
            pltpu.VMEM((rhs, unknowns), F32),
            pltpu.VMEM((2 * rhs, unknowns), F32),
            pltpu.VMEM((2 * rhs, unknowns), F32),
            pltpu.VMEM((rhs, unknowns), F32),
            pltpu.VMEM((rhs, unknowns), F32),
            pltpu.SemaphoreType.DMA((block_order.shape[2] + 4,)),
            pltpu.SemaphoreType.DMA((8,)),
            pltpu.SemaphoreType.DMA((8,)),
        ],
        compiler_params=pltpu.CompilerParams(
            collective_id=0, has_side_effects=True, vmem_limit_bytes=40 * 1024 * 1024
        ),
        name="sketch_solve",
    )(*(pltpu.with_memory_space_constraint(v, pltpu.HBM) for v in given))
    residual = jnp.dot(
        solved.astype(BF16), near_design, preferred_element_type=F32
    ) - near_targets.astype(F32)
    return (solved.T, residual)


def solution(mesh):
    return jax.shard_map(
        on_device,
        mesh=mesh,
        in_specs=(
            P(None, "rows"),
            P("cols", "rows"),
            P(None, "rows"),
            P(None, "rows"),
            P(None, "rows", None),
        ),
        out_specs=(P(None, "cols"), P("cols", "rows")),
        check_vma=False,
    )
```

```python
import functools
import math

import jax
import jax.numpy as jnp
from jax import lax
from jax.experimental import pallas as pl
from jax.experimental.pallas import tpu as pltpu
from jax.sharding import PartitionSpec as P

MESH = pl.DeviceIdType.MESH
F32 = jnp.float32
BF16 = jnp.bfloat16
NB = 32
NT = (((1,), (1,)), ((), ()))
TN = (((0,), (0,)), ((), ()))
HIGHEST = lax.Precision.HIGHEST


def parity_sign(bits):
    bits = bits ^ (bits >> 4)
    bits = bits ^ (bits >> 2)
    bits = (bits ^ (bits >> 1)) & 1
    return (1 - 2 * bits).astype(F32)


def split(x):
    hi = x.astype(BF16)
    return hi, (x - hi.astype(F32)).astype(BF16)


def lane_of(tile, c):
    return jnp.broadcast_to(tile[:, c : c + 1], (8, 128))


def row_of(tile, j):
    return jnp.broadcast_to(tile[j : j + 1, :], (8, 128))


def tree(terms):
    while len(terms) > 1:
        paired = [terms[i] + terms[i + 1] for i in range(0, len(terms) - 1, 2)]
        terms = paired + ([terms[-1]] if len(terms) % 2 else [])
    return terms[0]


def small_inverse(cols, sub):
    for q in range(0, 8, 2):
        a, b, c = row_of(cols[q], q), row_of(cols[q + 1], q), row_of(cols[q + 1], q + 1)
        r = 1.0 / (a * c - b * b)
        t0, t1 = cols[q] * c - cols[q + 1] * b, cols[q + 1] * a - cols[q] * b
        t0 = jnp.where(sub == q, -c, jnp.where(sub == q + 1, b, t0))
        t1 = jnp.where(sub == q, b, jnp.where(sub == q + 1, -a, t1))
        fresh = []
        for j in range(8):
            if j == q:
                fresh.append(-(r * t0))
            elif j == q + 1:
                fresh.append(-(r * t1))
            else:
                kept = jnp.where((sub == q) | (sub == q + 1), 0.0, cols[j])
                fresh.append(kept - r * (t0 * row_of(cols[j], q) + t1 * row_of(cols[j], q + 1)))
        cols = fresh
    return cols


def eliminate(tiles, k0, sub, lane):
    home = k0 // 128
    groups = NB // 8
    ahead = None
    for s in range(groups):
        c0 = k0 + 8 * s - 128 * home
        diagonal = ahead or [lane_of(tiles[s][home], c0 + j) for j in range(8)]
        inverse = small_inverse(diagonal, sub)
        if s + 1 < groups:
            low = [lane_of(tiles[s + 1][home], c0 + j) for j in range(8)]
            after = [lane_of(tiles[s + 1][home], c0 + 8 + j) for j in range(8)]
            scaled = [
                tree([low[i] * row_of(inverse[j], i) for i in range(8)]) for j in range(8)
            ]
            ahead = [
                after[j] - tree([scaled[i] * row_of(low[i], j) for i in range(8)])
                for j in range(8)
            ]
        cols = [
            [diagonal[j] if g == s else lane_of(tiles[g][home], c0 + j) for g in range(groups)]
            for j in range(8)
        ]
        inside = (lane >= c0) & (lane < c0 + 8)
        unit = jnp.where(lane == sub + c0, 1.0, 0.0)
        lead = [jnp.where(inside, unit, t) if h == home else t for h, t in enumerate(tiles[s])]
        fresh = [tree([inverse[j] * row_of(lead[h], j) for j in range(8)]) for h in range(2)]
        rows = [[row_of(fresh[h], j) for j in range(8)] for h in range(2)]
        moved = [None] * groups
        moved[s] = fresh
        for g in [(s + d) % groups for d in range(1, groups)]:
            line = [None, None]
            for h in (home, 1 - home):
                kept = jnp.where(inside, 0.0, tiles[g][h]) if h == home else tiles[g][h]
                line[h] = kept - tree([cols[j][g] * rows[h][j] for j in range(8)])
            moved[g] = line
        tiles = moved
    return tiles


def invert(mat, after_round):
    n = mat.shape[0]
    sub = lax.broadcasted_iota(jnp.int32, (8, 128), 0)
    lane = lax.broadcasted_iota(jnp.int32, (8, 128), 1)
    wide = lax.broadcasted_iota(jnp.int32, (NB, n), 1)
    panel = mat[0:NB, :]
    for k0 in range(0, n, NB):
        k1 = k0 + NB
        left_hi, left_lo = split(jnp.where(wide < k0, -panel, panel))
        left = jnp.concatenate([left_hi, left_hi, left_lo], axis=0)
        tiles = [
            [panel[8 * g : 8 * g + 8, 128 * h : 128 * h + 128] for h in range(2)]
            for g in range(NB // 8)
        ]
        tiles = eliminate(tiles, k0, sub, lane)
        done = jnp.concatenate([jnp.concatenate(t, axis=1) for t in tiles], axis=0)
        right_hi, right_lo = split(done)
        right = jnp.concatenate([right_hi, right_lo, right_hi], axis=0)
        inside = (wide >= k0) & (wide < k1)
        if k1 < n:
            first = lax.dot_general(left[:, k1 : k1 + NB], right, TN, preferred_element_type=F32)
            panel = jnp.where(inside, 0.0, mat[k1 : k1 + NB, :]) - first
        update = lax.dot_general(left, right, TN, preferred_element_type=F32)
        for other in range(0, n, NB):
            here = slice(other, other + NB)
            if other == k0:
                mat[here, :] = done
            elif other != k1:
                mat[here, :] = jnp.where(inside, 0.0, mat[here, :]) - update[here, :]
        after_round(k0 // NB)


def kernel(
    order_ref,
    design_ref,
    targets_ref,
    flips_ref,
    listed_ref,
    out_ref,
    dv,
    tv,
    order,
    fv,
    lv,
    walsh,
    srcs,
    lhs_a,
    lhs_b,
    acc,
    acc_e,
    xs,
    xe,
    rs_s,
    rs_e,
    sf,
    ef,
    mat,
    gmat,
    bt,
    b_near,
    xsend,
    xrecv,
    ysend,
    yrecv,
    in_sems,
    send_sems,
    recv_sems,
):
    unknowns = dv.shape[0]
    rows_here = dv.shape[1]
    block_len = walsh.shape[1]
    blocks = rows_here // block_len
    steps = 2
    picks = 128
    inv_root = 1.0 / math.sqrt(block_len)
    keep_scale = math.sqrt(rows_here / listed_ref.shape[1])
    row = lax.axis_index("rows")
    col = lax.axis_index("cols")
    core = row % 2
    xy = (row // 2) % 16
    z_lo = row // 32
    z = col * 2 + z_lo

    def chunk_copy(b):
        lanes = pl.ds(b * block_len, block_len)
        return pltpu.make_async_copy(design_ref.at[:, lanes], dv.at[:, lanes], in_sems.at[b])

    small = (
        pltpu.make_async_copy(order_ref, order, in_sems.at[blocks + 3]),
        pltpu.make_async_copy(listed_ref, lv, in_sems.at[blocks]),
        pltpu.make_async_copy(flips_ref, fv, in_sems.at[blocks + 1]),
        pltpu.make_async_copy(targets_ref, tv, in_sems.at[blocks + 2]),
    )
    small[0].start()
    small[1].start()
    small[2].start()
    chunk_copy(0).start()
    small[3].start()
    for b in range(1, blocks):
        chunk_copy(b).start()

    barrier = pltpu.get_barrier_semaphore()

    def z_peer(k):
        other = (z + k) % 8
        return ((other % 2) * 32 + row % 32, other // 2)

    for mask in range(1, 64):
        pl.semaphore_signal(barrier, inc=1, device_id=(row ^ mask, col), device_id_type=MESH)

    for k in range(1, 8):

        @pl.when(((z + k) % 8) // 2 != col)
        def _():
            pl.semaphore_signal(barrier, inc=1, device_id=z_peer(k), device_id_type=MESH)

    small[0].wait()
    small[1].wait()
    picked = lv[:, pl.ds(pl.multiple_of(col * picks, picks), picks)]
    eye = lax.broadcasted_iota(jnp.int32, (picks, picks), 0) == lax.broadcasted_iota(
        jnp.int32, (picks, picks), 1
    )
    for t in range(steps):
        line = picked[t : t + 1, :]
        target_block = line // block_len
        source = jnp.zeros_like(line)
        for b in range(blocks):
            source = jnp.where(target_block == b, order[t, b], source)
        code = (source * block_len + line % block_len).astype(F32)
        column = jnp.sum(
            jnp.where(eye, jnp.broadcast_to(code, (picks, picks)), 0.0), axis=1, keepdims=True
        ).astype(jnp.int32)
        srcs[t * picks : (t + 1) * picks, :] = jnp.broadcast_to(column // block_len, (picks, 128))
        within = column % block_len
        low = parity_sign(within & lax.broadcasted_iota(jnp.int32, (picks, 128), 1)).astype(BF16)
        high = jnp.broadcast_to(within // 128, (picks, 128))
        for h in range(block_len // 128):
            walsh[t * picks : (t + 1) * picks, h * 128 : (h + 1) * 128] = low * parity_sign(
                high & h
            ).astype(BF16)
    small[2].wait()
    width = 2 * block_len
    acc[...] = jnp.zeros_like(acc)

    def build(pair, lhs):
        for b in range(2):
            here = pl.ds(pl.multiple_of(pair * width, width) + b * block_len, block_len)
            for t in range(steps):
                own = slice(t * picks, (t + 1) * picks)
                sign = (2 * fv[t : t + 1, here] - 1).astype(F32).astype(BF16)
                chosen = jnp.where(srcs[own, :] == 2 * pair + b, 1.0, 0.0).astype(BF16)
                for h in range(block_len // 128):
                    part = slice(h * 128, (h + 1) * 128)
                    place = slice(b * block_len + h * 128, b * block_len + (h + 1) * 128)
                    lhs[own, place] = walsh[own, part] * chosen * sign[:, part]

    def apply(pair, lhs):
        lanes = pl.ds(pl.multiple_of(pair * width, width), width)
        acc[...] += lax.dot_general(lhs[...], dv[:, lanes], NT, preferred_element_type=F32)

    def arrived(pair):
        for b in range(2):
            here = pl.ds(pl.multiple_of(pair * width, width) + b * block_len, block_len)
            pltpu.make_async_copy(
                design_ref.at[:, here], dv.at[:, here], in_sems.at[2 * pair + b]
            ).wait()

    build(0, lhs_a)

    @pl.loop(0, blocks // 4)
    def _(quad):
        arrived(2 * quad)
        arrived(2 * quad + 1)
        build(2 * quad + 1, lhs_b)
        apply(2 * quad, lhs_a)
        build(jnp.minimum(2 * quad + 2, blocks // 2 - 1), lhs_a)
        apply(2 * quad + 1, lhs_b)

    for half in range(2):
        lanes = slice(half * 128, (half + 1) * 128)
        for rb in range(16):
            for t in range(steps):
                first = t * picks + rb * 8
                tile = (acc[first : first + 8, lanes] * inv_root).astype(BF16)
                xs[2 * (half * 16 + rb) + t] = tile.astype(F32) * keep_scale

    pl.semaphore_wait(barrier, 63 + 6)

    def remote(src, dst, stage, peer):
        return pltpu.make_async_remote_copy(
            src_ref=src,
            dst_ref=dst,
            send_sem=send_sems.at[stage],
            recv_sem=recv_sems.at[stage],
            device_id=peer,
            device_id_type=MESH,
        )

    def hops(mask):
        ring = (0, 1, 2, 1)
        return (mask >> 5) + ring[mask >> 3 & 3] + ring[mask >> 1 & 3]

    def scatter(src, dst, stage):
        for mask in sorted(range(1, 64), key=lambda m: (-hops(m), m)):
            peer = row ^ mask
            remote(src.at[peer], dst.at[mask - 1], stage, (peer, col)).start()

    plane = sorted(range(1, 16), key=lambda m: (-hops(2 * m), m))

    def gather_z(full, stage):
        for k in (4, 3, 5, 2, 6, 1, 7):
            place = full.at[z, xy]
            remote(place, place, stage, z_peer(k)).start()

    def gather_xy(full, stage):
        for mask in plane:
            place = full.at[:, xy]
            peer = row ^ (2 * mask)
            remote(place, place, stage, (peer, col)).start()

    def all_of(buffer, stage):
        return remote(buffer, buffer, stage, (row, col))

    def total(own, parts):
        sums = [own]
        for lead in range(3):
            sums.append(parts[lead])
        for index in range(3, 63):
            sums[index % 4] = sums[index % 4] + parts[index]
        return (sums[0] + sums[1]) + (sums[2] + sums[3])

    scatter(xs, rs_s, 0)

    small[3].wait()
    acc_e[...] = jnp.zeros_like(acc_e)

    @pl.loop(0, blocks // 4)
    def _(part):
        lanes = pl.ds(pl.multiple_of(part * 2 * width, 2 * width), 2 * width)
        own = dv[pl.ds(pl.multiple_of(col * 64, 64), 64), lanes]
        both = jnp.concatenate([own, tv[:, lanes]], axis=0)
        acc_e[...] += lax.dot_general(both, dv[:, lanes], NT, preferred_element_type=F32)

    for half in range(2):
        lanes = slice(half * 128, (half + 1) * 128)
        for rb in range(16):
            xe[2 * (half * 16 + rb) + 1] = acc_e[rb * 4 : rb * 4 + 4, lanes]
            if rb < 8:
                xe[2 * (half * 16 + rb)] = acc_e[64 + rb * 4 : 68 + rb * 4, lanes]
            else:
                xe[2 * (half * 16 + rb)] = jnp.zeros((4, 128), F32)
    scatter(xe, rs_e, 1)
    all_of(rs_s, 0).wait_recv()
    sf[z, xy] = total(xs[row], rs_s)
    near_first = (1, 7, 2, 6, 3, 5, 4)
    for k in reversed(near_first):
        place = sf.at[z, xy]
        remote(place, place, 7 + k, z_peer(k)).start()
    for k in (0,) + near_first:
        place = sf.at[(z + 8 - k) % 8, xy]
        if k:
            remote(place, place, 7 + k, z_peer(k)).wait_recv()
        for mask in plane:
            remote(place, place, 4, (row ^ (2 * mask), col)).start()

    all_of(rs_e, 1).wait_recv()
    ef[z, xy] = total(xe[row], rs_e)
    gather_z(ef, 3)
    all_of(sf.at[:, 0:15], 4).wait_recv()

    squares = jnp.zeros((8, 128), F32)
    halves = []
    for half in range(2):
        parts = [sf[2 * c + half].reshape(picks, 128) for c in range(4)]
        halves.append(jnp.concatenate(parts, axis=0))
    sketch = jnp.concatenate(halves, axis=1)
    for first in range(0, 512, 8):
        for lane in range(0, 256, 128):
            piece = sketch[first : first + 8, lane : lane + 128]
            squares = squares + piece * piece
    hi, lo = split(sketch)
    gram = lax.dot_general(hi, hi, TN, preferred_element_type=F32)
    gram = gram + lax.dot_general(hi, lo, TN, preferred_element_type=F32)
    gram = gram + lax.dot_general(lo, hi, TN, preferred_element_type=F32)
    shift = jnp.sum(squares) / unknowns
    diagonal = lax.broadcasted_iota(jnp.int32, (unknowns, unknowns), 0) == lax.broadcasted_iota(
        jnp.int32, (unknowns, unknowns), 1
    )
    unscale = 1.0 / shift
    mat[...] = gram * unscale + jnp.where(diagonal, 1.0, 0.0)

    def after_round(done):
        if done == 0:
            all_of(rs_e.at[0:7], 3).wait_recv()
            gather_xy(ef, 5)
        if done == 6:
            all_of(ef.at[:, 0:15], 5).wait_recv()
            for half in range(2):
                lanes = slice(half * 128, (half + 1) * 128)
                for rb in range(8):
                    bt[rb * 4 : rb * 4 + 4, lanes] = ef[2 * col + half, rb]
                for c in range(4):
                    for rb in range(16):
                        first = c * 64 + rb * 4
                        gmat[first : first + 4, lanes] = ef[2 * c + half, rb]

            @pl.when(core == 0)
            def _():
                remote(bt, b_near, 15, (row + 1, col)).start()

    invert(mat, after_round)

    inverse_hi, inverse_lo = split(mat[...] * unscale)

    def times_inverse(value):
        hi, lo = split(value)
        out = jnp.dot(hi, inverse_hi, preferred_element_type=F32)
        out = out + jnp.dot(lo, inverse_hi, preferred_element_type=F32)
        return out + jnp.dot(hi, inverse_lo, preferred_element_type=F32)

    @pl.when(core == 0)
    def _():
        xsend[...] = times_inverse(bt[...])
        handed = remote(xsend, xrecv, 6, (row + 1, col))
        handed.start()
        remote(ysend, yrecv, 7, (row + 1, col)).wait_recv()
        out_ref[...] = yrecv[...]
        handed.wait_send()
        remote(bt, b_near, 15, (row + 1, col)).wait_send()

    @pl.when(core == 1)
    def _():
        remote(bt, b_near, 15, (row - 1, col)).wait_recv()
        pull = times_inverse(b_near[...])
        turn_hi, turn_lo = split(times_inverse(gmat[...]))
        remote(xsend, xrecv, 6, (row - 1, col)).wait_recv()
        start = xrecv[...]
        rounded = start.astype(BF16)
        moved = jnp.dot(rounded, turn_hi, preferred_element_type=F32)
        moved = moved + jnp.dot(rounded, turn_lo, preferred_element_type=F32)
        moved = start + (pull - moved)
        ysend[...] = moved
        handed = remote(ysend, yrecv, 7, (row - 1, col))
        handed.start()
        out_ref[...] = moved
        handed.wait_send()

    all_of(rs_s, 0).wait_send()
    all_of(rs_e, 1).wait_send()
    for k in near_first:
        remote(rs_s.at[0], rs_s.at[0], 7 + k, z_peer(k)).wait_send()
    all_of(rs_e.at[0:7], 3).wait_send()
    all_of(sf.at[:, 0:15], 4).wait_send()
    all_of(ef.at[:, 0:15], 5).wait_send()


def residual_kernel(solved_ref, design_ref, targets_ref, solution_ref, residual_ref, parts, sems):
    pieces = parts.shape[0]
    width = parts.shape[2]
    rounded = solved_ref[...].astype(BF16)
    solution_copy = pltpu.make_async_copy(solved_ref, solution_ref, sems.at[pieces])
    solution_copy.start()
    copies = []
    for piece in range(pieces):
        lanes = slice(piece * width, (piece + 1) * width)
        product = jnp.dot(rounded, design_ref[:, lanes], preferred_element_type=F32)
        parts[piece] = product - targets_ref[:, lanes].astype(F32)
        copies.append(
            pltpu.make_async_copy(parts.at[piece], residual_ref.at[:, lanes], sems.at[piece])
        )
        copies[-1].start()
    for copy in copies:
        copy.wait()
    solution_copy.wait()


def on_device(design, targets, flip_bits, listed, block_order):
    unknowns, rows_here = design.shape
    block_len = rows_here // block_order.shape[2]
    rhs = targets.shape[0]
    order = block_order.reshape(2, block_order.shape[2])
    given = (order, design, targets, flip_bits, listed)
    solved, near_design, near_targets = pl.pallas_call(
        kernel,
        out_shape=(
            jax.ShapeDtypeStruct((rhs, unknowns), F32),
            jax.ShapeDtypeStruct(design.shape, BF16),
            jax.ShapeDtypeStruct(targets.shape, BF16),
        ),
        in_specs=[pl.BlockSpec(memory_space=pltpu.HBM)] * 5,
        out_specs=[pl.BlockSpec(memory_space=pltpu.VMEM)] * 3,
        scratch_shapes=[
            pltpu.SMEM((2, block_order.shape[2]), jnp.int32),
            pltpu.VMEM((2, rows_here), jnp.int32),
            pltpu.VMEM((2, 512), jnp.int32),
            pltpu.VMEM((256, block_len), BF16),
            pltpu.VMEM((256, 128), jnp.int32),
            pltpu.VMEM((256, 2 * block_len), BF16),
            pltpu.VMEM((256, 2 * block_len), BF16),
            pltpu.VMEM((256, unknowns), F32),
            pltpu.VMEM((96, unknowns), F32),
            pltpu.VMEM((64, 8, 128), F32),
            pltpu.VMEM((64, 4, 128), F32),
            pltpu.VMEM((63, 8, 128), F32),
            pltpu.VMEM((63, 4, 128), F32),
            pltpu.VMEM((8, 16, 8, 128), F32),
            pltpu.VMEM((8, 16, 4, 128), F32),
            pltpu.VMEM((unknowns, unknowns), F32),
            pltpu.VMEM((unknowns, unknowns), F32),
            pltpu.VMEM((rhs, unknowns), F32),
            pltpu.VMEM((rhs, unknowns), F32),
            pltpu.VMEM((rhs, unknowns), F32),
            pltpu.VMEM((rhs, unknowns), F32),
            pltpu.VMEM((rhs, unknowns), F32),
            pltpu.VMEM((rhs, unknowns), F32),
            pltpu.SemaphoreType.DMA((block_order.shape[2] + 4,)),
            pltpu.SemaphoreType.DMA((16,)),
            pltpu.SemaphoreType.DMA((16,)),
        ],
        compiler_params=pltpu.CompilerParams(
            collective_id=0, has_side_effects=True, vmem_limit_bytes=40 * 1024 * 1024
        ),
        name="sketch_solve",
    )(*(pltpu.with_memory_space_constraint(v, pltpu.HBM) for v in given))
    out, residual = pl.pallas_call(
        residual_kernel,
        out_shape=(
            jax.ShapeDtypeStruct((rhs, unknowns), F32),
            jax.ShapeDtypeStruct(targets.shape, F32),
        ),
        in_specs=[pl.BlockSpec(memory_space=pltpu.VMEM)] * 3,
        out_specs=[pl.BlockSpec(memory_space=pltpu.HBM)] * 2,
        scratch_shapes=[
            pltpu.VMEM((8, rhs, rows_here // 8), F32),
            pltpu.SemaphoreType.DMA((9,)),
        ],
        compiler_params=pltpu.CompilerParams(vmem_limit_bytes=16 * 1024 * 1024),
        name="residual",
    )(solved, near_design, near_targets)
    return (out.T, residual)


def solution(mesh):
    return jax.shard_map(
        on_device,
        mesh=mesh,
        in_specs=(
            P(None, "rows"),
            P("cols", "rows"),
            P(None, "rows"),
            P(None, "rows"),
            P(None, "rows", None),
        ),
        out_specs=(P(None, "cols"), P("cols", "rows")),
        check_vma=False,
    )
```

```python
import functools
import math

import jax
import jax.numpy as jnp
from jax import lax
from jax.experimental import pallas as pl
from jax.experimental.pallas import tpu as pltpu
from jax.sharding import PartitionSpec as P

MESH = pl.DeviceIdType.MESH
F32 = jnp.float32
BF16 = jnp.bfloat16
NB = 16
NT = (((1,), (1,)), ((), ()))
TN = (((0,), (0,)), ((), ()))
NN = (((1,), (0,)), ((), ()))
HIGHEST = lax.Precision.HIGHEST


def parity_sign(bits):
    bits = bits ^ (bits >> 4)
    bits = bits ^ (bits >> 2)
    bits = (bits ^ (bits >> 1)) & 1
    return (1 - 2 * bits).astype(F32)


def product(a, b, dims):
    (a_hi, a_lo), (b_hi, b_lo) = split(a), split(b)
    out = lax.dot_general(a_hi, b_hi, dims, preferred_element_type=F32)
    out = out + lax.dot_general(a_hi, b_lo, dims, preferred_element_type=F32)
    return out + lax.dot_general(a_lo, b_hi, dims, preferred_element_type=F32)


def split(x):
    hi = x.astype(BF16)
    return hi, (x - hi.astype(F32)).astype(BF16)


def lane_of(tile, c):
    return jnp.broadcast_to(tile[:, c : c + 1], (8, 128))


def row_of(tile, j):
    return jnp.broadcast_to(tile[j : j + 1, :], (8, 128))


def tree(terms):
    while len(terms) > 1:
        paired = [terms[i] + terms[i + 1] for i in range(0, len(terms) - 1, 2)]
        terms = paired + ([terms[-1]] if len(terms) % 2 else [])
    return terms[0]


def small_inverse(cols, sub):
    for q in range(0, 8, 2):
        a, b, c = row_of(cols[q], q), row_of(cols[q + 1], q), row_of(cols[q + 1], q + 1)
        r = 1.0 / (a * c - b * b)
        t0, t1 = cols[q] * c - cols[q + 1] * b, cols[q + 1] * a - cols[q] * b
        t0 = jnp.where(sub == q, -c, jnp.where(sub == q + 1, b, t0))
        t1 = jnp.where(sub == q, b, jnp.where(sub == q + 1, -a, t1))
        fresh = []
        for j in range(8):
            if j == q:
                fresh.append(-(r * t0))
            elif j == q + 1:
                fresh.append(-(r * t1))
            else:
                kept = jnp.where((sub == q) | (sub == q + 1), 0.0, cols[j])
                fresh.append(kept - r * (t0 * row_of(cols[j], q) + t1 * row_of(cols[j], q + 1)))
        cols = fresh
    return cols


def eliminate(tiles, k0, sub, lane):
    home = k0 // 128
    groups = NB // 8
    ahead = None
    for s in range(groups):
        c0 = k0 + 8 * s - 128 * home
        diagonal = ahead or [lane_of(tiles[s][home], c0 + j) for j in range(8)]
        inverse = small_inverse(diagonal, sub)
        if s + 1 < groups:
            low = [lane_of(tiles[s + 1][home], c0 + j) for j in range(8)]
            after = [lane_of(tiles[s + 1][home], c0 + 8 + j) for j in range(8)]
            scaled = [
                tree([low[i] * row_of(inverse[j], i) for i in range(8)]) for j in range(8)
            ]
            ahead = [
                after[j] - tree([scaled[i] * row_of(low[i], j) for i in range(8)])
                for j in range(8)
            ]
        cols = [
            [diagonal[j] if g == s else lane_of(tiles[g][home], c0 + j) for g in range(groups)]
            for j in range(8)
        ]
        inside = (lane >= c0) & (lane < c0 + 8)
        unit = jnp.where(lane == sub + c0, 1.0, 0.0)
        lead = [jnp.where(inside, unit, t) if h == home else t for h, t in enumerate(tiles[s])]
        fresh = [tree([inverse[j] * row_of(t, j) for j in range(8)]) for t in lead]
        rows = [[row_of(t, j) for j in range(8)] for t in fresh]
        moved = [None] * groups
        moved[s] = fresh
        for g in [(s + d) % groups for d in range(1, groups)]:
            line = []
            for h, tile in enumerate(tiles[g]):
                kept = jnp.where(inside, 0.0, tile) if h == home else tile
                line.append(kept - tree([cols[j][g] * rows[h][j] for j in range(8)]))
            moved[g] = line
        tiles = moved
    return tiles


def invert(mat, after_round):
    n = mat.shape[0]
    sub = lax.broadcasted_iota(jnp.int32, (8, 128), 0)
    lane = lax.broadcasted_iota(jnp.int32, (8, 128), 1)
    wide = lax.broadcasted_iota(jnp.int32, (NB, n), 1)
    panel = mat[0:NB, :]
    for k0 in range(0, n, NB):
        k1 = k0 + NB
        left_hi, left_lo = split(jnp.where(wide < k0, -panel, panel))
        left = jnp.concatenate([left_hi, left_hi, left_lo], axis=0)
        tiles = [
            [panel[8 * g : 8 * g + 8, lane0 : lane0 + 128] for lane0 in range(0, n, 128)]
            for g in range(NB // 8)
        ]
        tiles = eliminate(tiles, k0, sub, lane)
        done = jnp.concatenate([jnp.concatenate(t, axis=1) for t in tiles], axis=0)
        right_hi, right_lo = split(done)
        right = jnp.concatenate([right_hi, right_lo, right_hi], axis=0)
        inside = (wide >= k0) & (wide < k1)
        if k1 < n:
            first = lax.dot_general(left[:, k1 : k1 + NB], right, TN, preferred_element_type=F32)
            panel = jnp.where(inside, 0.0, mat[k1 : k1 + NB, :]) - first
        update = lax.dot_general(left, right, TN, preferred_element_type=F32)
        for other in range(0, n, NB):
            here = slice(other, other + NB)
            if other == k0:
                mat[here, :] = done
            elif other != k1:
                mat[here, :] = jnp.where(inside, 0.0, mat[here, :]) - update[here, :]
        after_round(k0 // NB)


def kernel(
    order_ref,
    design_ref,
    targets_ref,
    flips_ref,
    listed_ref,
    out_ref,
    dv,
    tv,
    order,
    fv,
    lv,
    walsh,
    srcs,
    lhs_a,
    lhs_b,
    acc,
    acc_e,
    xs,
    xe,
    rs_s,
    rs_e,
    sf,
    ef,
    mat,
    gmat,
    bt,
    start_at,
    last,
    top,
    tail,
    ratio_ref,
    sums,
    in_sems,
    send_sems,
    recv_sems,
):
    unknowns = dv.shape[0]
    rows_here = dv.shape[1]
    block_len = walsh.shape[1]
    blocks = rows_here // block_len
    steps = 2
    picks = 128
    inv_root = 1.0 / math.sqrt(block_len)
    keep_scale = math.sqrt(rows_here / listed_ref.shape[1])
    row = lax.axis_index("rows")
    col = lax.axis_index("cols")
    core = row % 2
    xy = (row // 2) % 16
    z_lo = row // 32
    z = col * 2 + z_lo

    def chunk_copy(b):
        lanes = pl.ds(b * block_len, block_len)
        return pltpu.make_async_copy(design_ref.at[:, lanes], dv.at[:, lanes], in_sems.at[b])

    small = (
        pltpu.make_async_copy(order_ref, order, in_sems.at[blocks + 3]),
        pltpu.make_async_copy(listed_ref, lv, in_sems.at[blocks]),
        pltpu.make_async_copy(flips_ref, fv, in_sems.at[blocks + 1]),
        pltpu.make_async_copy(targets_ref, tv, in_sems.at[blocks + 2]),
    )
    small[0].start()
    small[1].start()
    small[2].start()
    chunk_copy(0).start()
    small[3].start()
    for b in range(1, blocks):
        chunk_copy(b).start()

    barrier = pltpu.get_barrier_semaphore()

    def z_peer(k):
        other = (z + k) % 8
        return ((other % 2) * 32 + row % 32, other // 2)

    for mask in range(1, 64):
        pl.semaphore_signal(barrier, inc=1, device_id=(row ^ mask, col), device_id_type=MESH)

    for k in range(1, 8):

        @pl.when(((z + k) % 8) // 2 != col)
        def _():
            pl.semaphore_signal(barrier, inc=1, device_id=z_peer(k), device_id_type=MESH)

    small[0].wait()
    small[1].wait()
    picked = lv[:, pl.ds(pl.multiple_of(col * picks, picks), picks)]
    eye = lax.broadcasted_iota(jnp.int32, (picks, picks), 0) == lax.broadcasted_iota(
        jnp.int32, (picks, picks), 1
    )
    for t in range(steps):
        line = picked[t : t + 1, :]
        target_block = line // block_len
        source = jnp.zeros_like(line)
        for b in range(blocks):
            source = jnp.where(target_block == b, order[t, b], source)
        code = (source * block_len + line % block_len).astype(F32)
        column = jnp.sum(
            jnp.where(eye, jnp.broadcast_to(code, (picks, picks)), 0.0), axis=1, keepdims=True
        ).astype(jnp.int32)
        srcs[t * picks : (t + 1) * picks, :] = jnp.broadcast_to(column // block_len, (picks, 128))
        within = column % block_len
        low = parity_sign(within & lax.broadcasted_iota(jnp.int32, (picks, 128), 1)).astype(BF16)
        high = jnp.broadcast_to(within // 128, (picks, 128))
        for h in range(block_len // 128):
            walsh[t * picks : (t + 1) * picks, h * 128 : (h + 1) * 128] = low * parity_sign(
                high & h
            ).astype(BF16)
    small[2].wait()
    width = 2 * block_len
    acc[...] = jnp.zeros_like(acc)

    def build(pair, lhs):
        for b in range(2):
            here = pl.ds(pl.multiple_of(pair * width, width) + b * block_len, block_len)
            for t in range(steps):
                own = slice(t * picks, (t + 1) * picks)
                sign = (2 * fv[t : t + 1, here] - 1).astype(F32).astype(BF16)
                chosen = jnp.where(srcs[own, :] == 2 * pair + b, 1.0, 0.0).astype(BF16)
                for h in range(block_len // 128):
                    part = slice(h * 128, (h + 1) * 128)
                    place = slice(b * block_len + h * 128, b * block_len + (h + 1) * 128)
                    lhs[own, place] = walsh[own, part] * chosen * sign[:, part]

    def apply(pair, lhs):
        lanes = pl.ds(pl.multiple_of(pair * width, width), width)
        acc[...] += lax.dot_general(lhs[...], dv[:, lanes], NT, preferred_element_type=F32)

    def arrived(pair):
        for b in range(2):
            here = pl.ds(pl.multiple_of(pair * width, width) + b * block_len, block_len)
            pltpu.make_async_copy(
                design_ref.at[:, here], dv.at[:, here], in_sems.at[2 * pair + b]
            ).wait()

    build(0, lhs_a)

    @pl.loop(0, blocks // 4)
    def _(quad):
        arrived(2 * quad)
        arrived(2 * quad + 1)
        build(2 * quad + 1, lhs_b)
        apply(2 * quad, lhs_a)
        build(jnp.minimum(2 * quad + 2, blocks // 2 - 1), lhs_a)
        apply(2 * quad + 1, lhs_b)

    for half in range(2):
        lanes = slice(half * 128, (half + 1) * 128)
        for rb in range(16):
            for t in range(steps):
                first = t * picks + rb * 8
                tile = (acc[first : first + 8, lanes] * inv_root).astype(BF16)
                xs[2 * (half * 16 + rb) + t] = tile.astype(F32) * keep_scale

    pl.semaphore_wait(barrier, 63 + 6)

    def remote(src, dst, stage, peer):
        return pltpu.make_async_remote_copy(
            src_ref=src,
            dst_ref=dst,
            send_sem=send_sems.at[stage],
            recv_sem=recv_sems.at[stage],
            device_id=peer,
            device_id_type=MESH,
        )

    def hops(mask):
        ring = (0, 1, 2, 1)
        return (mask >> 5) + ring[mask >> 3 & 3] + ring[mask >> 1 & 3]

    def scatter(src, dst, stage):
        for mask in sorted(range(1, 64), key=lambda m: (-hops(m), m)):
            peer = row ^ mask
            remote(src.at[peer], dst.at[mask - 1], stage, (peer, col)).start()

    plane = sorted(range(1, 16), key=lambda m: (-hops(2 * m), m))

    def gather_z(full, stage):
        for k in (4, 3, 5, 2, 6, 1, 7):
            place = full.at[z, xy]
            remote(place, place, stage, z_peer(k)).start()

    def gather_xy(full, stage):
        for mask in plane:
            place = full.at[:, xy]
            peer = row ^ (2 * mask)
            remote(place, place, stage, (peer, col)).start()

    def all_of(buffer, stage):
        return remote(buffer, buffer, stage, (row, col))

    def total(own, parts):
        lines = [own] + [parts[lead] for lead in range(3)]
        for index in range(3, 63):
            lines[index % 4] = lines[index % 4] + parts[index]
        return (lines[0] + lines[1]) + (lines[2] + lines[3])

    scatter(xs, rs_s, 0)

    small[3].wait()
    acc_e[...] = jnp.zeros_like(acc_e)

    @pl.loop(0, blocks // 4)
    def _(part):
        lanes = pl.ds(pl.multiple_of(part * 2 * width, 2 * width), 2 * width)
        own = dv[pl.ds(pl.multiple_of(col * 64, 64), 64), lanes]
        both = jnp.concatenate([own, tv[:, lanes]], axis=0)
        acc_e[...] += lax.dot_general(both, dv[:, lanes], NT, preferred_element_type=F32)

    for half in range(2):
        lanes = slice(half * 128, (half + 1) * 128)
        for rb in range(16):
            xe[2 * (half * 16 + rb) + 1] = acc_e[rb * 4 : rb * 4 + 4, lanes]
            if rb < 8:
                xe[2 * (half * 16 + rb)] = acc_e[64 + rb * 4 : 68 + rb * 4, lanes]
            else:
                xe[2 * (half * 16 + rb)] = jnp.zeros((4, 128), F32)
    scatter(xe, rs_e, 1)
    all_of(rs_s, 0).wait_recv()
    sf[z, xy] = total(xs[row], rs_s)
    for k in (4, 3, 5, 2, 6, 1, 7):
        place = sf.at[z, xy]
        remote(place, place, 7 + k, z_peer(k)).start()

    def along_z(k):
        place = sf.at[(z + 8 - k) % 8, xy]
        if k:
            remote(place, place, 7 + k, z_peer(k)).wait_recv()

    def over_plane(k, stage):
        place = sf.at[(z + 8 - k) % 8, xy]
        for mask in plane:
            remote(place, place, stage, (row ^ (2 * mask), col)).start()

    even, odd = (0, 2, 6, 4), (1, 7, 3, 5)
    for parity, first, second in ((0, even, odd), (1, odd, even)):

        @pl.when(z_lo == parity)
        def _():
            for k in first:
                along_z(k)
                over_plane(k, 4)
            for k in second:
                along_z(k)

    sums[xy] = jnp.sum(
        tree([sf[i, xy] * sf[i, xy] for i in range(8)]), axis=0, keepdims=True
    )
    for mask in plane:
        remote(sums.at[xy], sums.at[xy], 17, (row ^ (2 * mask), col)).start()
    def send_rest(whose):
        for parity, second in ((0, odd), (1, even)):

            @pl.when((z_lo == parity) & (core == whose))
            def _():
                for k in second:
                    over_plane(k, 16)

    send_rest(0)
    all_of(rs_e, 1).wait_recv()
    ef[z, xy] = total(xe[row], rs_e)
    gather_z(ef, 3)
    all_of(sf.at[0:4, 0:15], 4).wait_recv()
    all_of(sums.at[0:15], 17).wait_recv()
    send_rest(1)

    def half_of(half):
        return jnp.concatenate([sf[2 * c + half].reshape(picks, 128) for c in range(4)], axis=0)

    shift = jnp.sum(tree([sums[i] for i in range(16)])) / unknowns
    unscale = 1.0 / shift
    unit = jnp.where(eye, 1.0, 0.0)
    first_half = half_of(0)
    top[...] = product(first_half, first_half, TN) * unscale + unit

    def after_top(done):
        if done == 1:
            all_of(rs_e.at[0:7], 3).wait_recv()
            gather_xy(ef, 5)

    def after_low(done):
        if done == 5:
            all_of(ef.at[:, 0:15], 5).wait_recv()

            @pl.when(core == 0)
            def _():
                for half in range(2):
                    lanes = slice(half * 128, (half + 1) * 128)
                    for rb in range(8):
                        bt[rb * 4 : rb * 4 + 4, lanes] = ef[2 * col + half, rb]
                remote(bt, bt, 15, (row + 1, col)).start()

            @pl.when(core == 1)
            def _():
                for half in range(2):
                    lanes = slice(half * 128, (half + 1) * 128)
                    for c in range(4):
                        for rb in range(16):
                            first = c * 64 + rb * 4
                            gmat[first : first + 4, lanes] = ef[2 * c + half, rb]
                remote(gmat, gmat, 18, (row - 1, col)).start()

    invert(top, after_top)
    all_of(sf.at[0:4, 0:15], 16).wait_recv()
    second_half = half_of(1)
    cross = product(half_of(0), second_half, TN) * unscale
    ratio = product(top[...], cross, NN)
    corner = product(second_half, second_half, TN) * unscale + unit
    tail[...] = corner - product(cross, ratio, TN)
    ratio_ref[...] = ratio
    invert(tail, after_low)
    ratio = ratio_ref[...]
    corner = tail[...]
    across = product(ratio, corner, NN)
    mat[0:128, 0:128] = (top[...] + product(across, ratio, NT)) * unscale
    mat[0:128, 128:256] = across * -unscale
    mat[128:256, 0:128] = product(corner, ratio, NT) * -unscale
    mat[128:256, 128:256] = corner * unscale

    @pl.when(core == 0)
    def _():
        start_at[...] = product(bt[...], mat[...], NN)
        remote(start_at, start_at, 6, (row + 1, col)).start()
        remote(gmat, gmat, 18, (row + 1, col)).wait_recv()

    @pl.when(core == 1)
    def _():
        last[...] = mat[...]
        remote(last, last, 7, (row - 1, col)).start()
        remote(bt, bt, 15, (row - 1, col)).wait_recv()
        remote(start_at, start_at, 6, (row - 1, col)).wait_recv()

    start = start_at[...]
    rounded = start.astype(BF16)
    gram_hi, gram_lo = split(gmat[...])
    gradient = jnp.dot(rounded, gram_hi, preferred_element_type=F32)
    gradient = gradient + jnp.dot(rounded, gram_lo, preferred_element_type=F32)
    gradient = gradient - bt[...]

    @pl.when(core == 0)
    def _():
        remote(last, last, 7, (row + 1, col)).wait_recv()

    out_ref[...] = start - product(gradient, last[...], NN)

    @pl.when(core == 0)
    def _():
        remote(start_at, start_at, 6, (row + 1, col)).wait_send()
        remote(bt, bt, 15, (row + 1, col)).wait_send()

    @pl.when(core == 1)
    def _():
        remote(last, last, 7, (row - 1, col)).wait_send()
        remote(gmat, gmat, 18, (row - 1, col)).wait_send()

    all_of(rs_s, 0).wait_send()
    all_of(rs_e, 1).wait_send()
    for k in range(1, 8):
        remote(rs_s.at[0], rs_s.at[0], 7 + k, z_peer(k)).wait_send()
    all_of(rs_e.at[0:7], 3).wait_send()
    all_of(sf.at[0:4, 0:15], 4).wait_send()
    all_of(sf.at[0:4, 0:15], 16).wait_send()
    all_of(sums.at[0:15], 17).wait_send()
    all_of(ef.at[:, 0:15], 5).wait_send()


def residual_kernel(solved_ref, design_ref, targets_ref, solution_ref, residual_ref, parts, sems):
    pieces = parts.shape[0]
    width = parts.shape[2]
    rounded = solved_ref[...].astype(BF16)
    solution_copy = pltpu.make_async_copy(solved_ref, solution_ref, sems.at[pieces])
    solution_copy.start()
    copies = []
    for piece in range(pieces):
        lanes = slice(piece * width, (piece + 1) * width)
        product = jnp.dot(rounded, design_ref[:, lanes], preferred_element_type=F32)
        parts[piece] = product - targets_ref[:, lanes].astype(F32)
        copies.append(
            pltpu.make_async_copy(parts.at[piece], residual_ref.at[:, lanes], sems.at[piece])
        )
        copies[-1].start()
    for copy in copies:
        copy.wait()
    solution_copy.wait()


def on_device(design, targets, flip_bits, listed, block_order):
    unknowns, rows_here = design.shape
    block_len = rows_here // block_order.shape[2]
    rhs = targets.shape[0]
    order = block_order.reshape(2, block_order.shape[2])
    given = (order, design, targets, flip_bits, listed)
    solved, near_design, near_targets = pl.pallas_call(
        kernel,
        out_shape=(
            jax.ShapeDtypeStruct((rhs, unknowns), F32),
            jax.ShapeDtypeStruct(design.shape, BF16),
            jax.ShapeDtypeStruct(targets.shape, BF16),
        ),
        in_specs=[pl.BlockSpec(memory_space=pltpu.HBM)] * 5,
        out_specs=[pl.BlockSpec(memory_space=pltpu.VMEM)] * 3,
        scratch_shapes=[
            pltpu.SMEM((2, block_order.shape[2]), jnp.int32),
            pltpu.VMEM((2, rows_here), jnp.int32),
            pltpu.VMEM((2, 512), jnp.int32),
            pltpu.VMEM((256, block_len), BF16),
            pltpu.VMEM((256, 128), jnp.int32),
            pltpu.VMEM((256, 2 * block_len), BF16),
            pltpu.VMEM((256, 2 * block_len), BF16),
            pltpu.VMEM((256, unknowns), F32),
            pltpu.VMEM((96, unknowns), F32),
            pltpu.VMEM((64, 8, 128), F32),
            pltpu.VMEM((64, 4, 128), F32),
            pltpu.VMEM((63, 8, 128), F32),
            pltpu.VMEM((63, 4, 128), F32),
            pltpu.VMEM((8, 16, 8, 128), F32),
            pltpu.VMEM((8, 16, 4, 128), F32),
            pltpu.VMEM((unknowns, unknowns), F32),
            pltpu.VMEM((unknowns, unknowns), F32),
            pltpu.VMEM((rhs, unknowns), F32),
            pltpu.VMEM((rhs, unknowns), F32),
            pltpu.VMEM((unknowns, unknowns), F32),
            pltpu.VMEM((128, 128), F32),
            pltpu.VMEM((128, 128), F32),
            pltpu.VMEM((128, 128), F32),
            pltpu.VMEM((16, 1, 128), F32),
            pltpu.SemaphoreType.DMA((block_order.shape[2] + 4,)),
            pltpu.SemaphoreType.DMA((19,)),
            pltpu.SemaphoreType.DMA((19,)),
        ],
        compiler_params=pltpu.CompilerParams(
            collective_id=0, has_side_effects=True, vmem_limit_bytes=40 * 1024 * 1024
        ),
        name="sketch_solve",
    )(*(pltpu.with_memory_space_constraint(v, pltpu.HBM) for v in given))
    out, residual = pl.pallas_call(
        residual_kernel,
        out_shape=(
            jax.ShapeDtypeStruct((rhs, unknowns), F32),
            jax.ShapeDtypeStruct(targets.shape, F32),
        ),
        in_specs=[pl.BlockSpec(memory_space=pltpu.VMEM)] * 3,
        out_specs=[pl.BlockSpec(memory_space=pltpu.HBM)] * 2,
        scratch_shapes=[
            pltpu.VMEM((8, rhs, rows_here // 8), F32),
            pltpu.SemaphoreType.DMA((9,)),
        ],
        compiler_params=pltpu.CompilerParams(vmem_limit_bytes=16 * 1024 * 1024),
        name="residual",
    )(solved, near_design, near_targets)
    return (out.T, residual)


def solution(mesh):
    return jax.shard_map(
        on_device,
        mesh=mesh,
        in_specs=(
            P(None, "rows"),
            P("cols", "rows"),
            P(None, "rows"),
            P(None, "rows"),
            P(None, "rows", None),
        ),
        out_specs=(P(None, "cols"), P("cols", "rows")),
        check_vma=False,
    )
```

```python
import functools
import math

import jax
import jax.numpy as jnp
from jax import lax
from jax.experimental import pallas as pl
from jax.experimental.pallas import tpu as pltpu
from jax.sharding import PartitionSpec as P

MESH = pl.DeviceIdType.MESH
F32 = jnp.float32
BF16 = jnp.bfloat16
NB = 16
NT = (((1,), (1,)), ((), ()))
TN = (((0,), (0,)), ((), ()))
NN = (((1,), (0,)), ((), ()))


def parity_sign(bits):
    bits = bits ^ (bits >> 4)
    bits = bits ^ (bits >> 2)
    bits = (bits ^ (bits >> 1)) & 1
    return (1 - 2 * bits).astype(F32)


def product(a, b, dims):
    (a_hi, a_lo), (b_hi, b_lo) = split(a), split(b)
    out = lax.dot_general(a_hi, b_hi, dims, preferred_element_type=F32)
    out = out + lax.dot_general(a_hi, b_lo, dims, preferred_element_type=F32)
    return out + lax.dot_general(a_lo, b_hi, dims, preferred_element_type=F32)


def split(x):
    hi = x.astype(BF16)
    return hi, (x - hi.astype(F32)).astype(BF16)


def lane_of(tile, c):
    return jnp.broadcast_to(tile[:, c : c + 1], (8, 128))


def row_of(tile, j):
    return jnp.broadcast_to(tile[j : j + 1, :], (8, 128))


def tree(terms):
    while len(terms) > 1:
        paired = [terms[i] + terms[i + 1] for i in range(0, len(terms) - 1, 2)]
        terms = paired + ([terms[-1]] if len(terms) % 2 else [])
    return terms[0]


def small_inverse(cols, sub):
    for q in range(0, 8, 2):
        a, b, c = row_of(cols[q], q), row_of(cols[q + 1], q), row_of(cols[q + 1], q + 1)
        r = 1.0 / (a * c - b * b)
        t0, t1 = cols[q] * c - cols[q + 1] * b, cols[q + 1] * a - cols[q] * b
        t0 = jnp.where(sub == q, -c, jnp.where(sub == q + 1, b, t0))
        t1 = jnp.where(sub == q, b, jnp.where(sub == q + 1, -a, t1))
        fresh = []
        for j in range(8):
            if j == q:
                fresh.append(-(r * t0))
            elif j == q + 1:
                fresh.append(-(r * t1))
            else:
                kept = jnp.where((sub == q) | (sub == q + 1), 0.0, cols[j])
                fresh.append(kept - r * (t0 * row_of(cols[j], q) + t1 * row_of(cols[j], q + 1)))
        cols = fresh
    return cols


def eliminate(tiles, k0, sub, lane):
    home = k0 // 128
    groups = NB // 8
    ahead = None
    for s in range(groups):
        c0 = k0 + 8 * s - 128 * home
        diagonal = ahead or [lane_of(tiles[s][home], c0 + j) for j in range(8)]
        inverse = small_inverse(diagonal, sub)
        if s + 1 < groups:
            low = [lane_of(tiles[s + 1][home], c0 + j) for j in range(8)]
            after = [lane_of(tiles[s + 1][home], c0 + 8 + j) for j in range(8)]
            scaled = [
                tree([low[i] * row_of(inverse[j], i) for i in range(8)]) for j in range(8)
            ]
            ahead = [
                after[j] - tree([scaled[i] * row_of(low[i], j) for i in range(8)])
                for j in range(8)
            ]
        cols = [
            [diagonal[j] if g == s else lane_of(tiles[g][home], c0 + j) for g in range(groups)]
            for j in range(8)
        ]
        inside = (lane >= c0) & (lane < c0 + 8)
        unit = jnp.where(lane == sub + c0, 1.0, 0.0)
        lead = [jnp.where(inside, unit, t) if h == home else t for h, t in enumerate(tiles[s])]
        fresh = [tree([inverse[j] * row_of(t, j) for j in range(8)]) for t in lead]
        rows = [[row_of(t, j) for j in range(8)] for t in fresh]
        moved = [None] * groups
        moved[s] = fresh
        for g in [(s + d) % groups for d in range(1, groups)]:
            line = []
            for h, tile in enumerate(tiles[g]):
                kept = jnp.where(inside, 0.0, tile) if h == home else tile
                line.append(kept - tree([cols[j][g] * rows[h][j] for j in range(8)]))
            moved[g] = line
        tiles = moved
    return tiles


def invert(mat, after_round):
    n = mat.shape[0]
    sub = lax.broadcasted_iota(jnp.int32, (8, 128), 0)
    lane = lax.broadcasted_iota(jnp.int32, (8, 128), 1)
    wide = lax.broadcasted_iota(jnp.int32, (NB, n), 1)
    panel = mat[0:NB, :]
    for k0 in range(0, n, NB):
        k1 = k0 + NB
        left_hi, left_lo = split(jnp.where(wide < k0, -panel, panel))
        left = jnp.concatenate([left_hi, left_hi, left_lo], axis=0)
        tiles = [
            [panel[8 * g : 8 * g + 8, lane0 : lane0 + 128] for lane0 in range(0, n, 128)]
            for g in range(NB // 8)
        ]
        tiles = eliminate(tiles, k0, sub, lane)
        done = jnp.concatenate([jnp.concatenate(t, axis=1) for t in tiles], axis=0)
        right_hi, right_lo = split(done)
        right = jnp.concatenate([right_hi, right_lo, right_hi], axis=0)
        inside = (wide >= k0) & (wide < k1)
        if k1 < n:
            first = lax.dot_general(left[:, k1 : k1 + NB], right, TN, preferred_element_type=F32)
            panel = jnp.where(inside, 0.0, mat[k1 : k1 + NB, :]) - first
        update = lax.dot_general(left, right, TN, preferred_element_type=F32)
        for other in range(0, n, NB):
            here = slice(other, other + NB)
            if other == k0:
                mat[here, :] = done
            elif other != k1:
                mat[here, :] = jnp.where(inside, 0.0, mat[here, :]) - update[here, :]
        after_round(k0 // NB)


def kernel(
    order_ref,
    design_ref,
    targets_ref,
    flips_ref,
    listed_ref,
    out_ref,
    dv,
    tv,
    order,
    fv,
    lv,
    walsh,
    srcs,
    lhs_a,
    lhs_b,
    acc,
    acc_e,
    xs,
    xe,
    rs_s,
    rs_e,
    sf,
    ef,
    cross_ref,
    own_b,
    lead_ref,
    rest_ref,
    gmat,
    bt,
    start_at,
    last,
    top,
    tail,
    ratio_ref,
    sums,
    in_sems,
    send_sems,
    recv_sems,
):
    unknowns = dv.shape[0]
    rows_here = dv.shape[1]
    block_len = walsh.shape[1]
    blocks = rows_here // block_len
    steps = 2
    picks = 128
    inv_root = 1.0 / math.sqrt(block_len)
    keep_scale = math.sqrt(rows_here / listed_ref.shape[1])
    row = lax.axis_index("rows")
    col = lax.axis_index("cols")
    core = row % 2
    xy = (row // 2) % 16
    z_lo = row // 32
    z = col * 2 + z_lo

    def chunk_copy(b):
        lanes = pl.ds(b * block_len, block_len)
        return pltpu.make_async_copy(design_ref.at[:, lanes], dv.at[:, lanes], in_sems.at[b])

    small = (
        pltpu.make_async_copy(order_ref, order, in_sems.at[blocks + 3]),
        pltpu.make_async_copy(listed_ref, lv, in_sems.at[blocks]),
        pltpu.make_async_copy(flips_ref, fv, in_sems.at[blocks + 1]),
        pltpu.make_async_copy(targets_ref, tv, in_sems.at[blocks + 2]),
    )
    small[0].start()
    small[1].start()
    small[2].start()
    chunk_copy(0).start()
    small[3].start()
    for b in range(1, blocks):
        chunk_copy(b).start()

    barrier = pltpu.get_barrier_semaphore()

    def z_peer(k):
        other = (z + k) % 8
        return ((other % 2) * 32 + row % 32, other // 2)

    for mask in range(1, 64):
        pl.semaphore_signal(barrier, inc=1, device_id=(row ^ mask, col), device_id_type=MESH)

    for mask in range(2, 8):
        other = z ^ mask
        peer = ((other % 2) * 32 + row % 32, other // 2)
        pl.semaphore_signal(barrier, inc=1, device_id=peer, device_id_type=MESH)

    small[0].wait()
    small[1].wait()
    picked = lv[:, pl.ds(pl.multiple_of(col * picks, picks), picks)]
    eye = lax.broadcasted_iota(jnp.int32, (picks, picks), 0) == lax.broadcasted_iota(
        jnp.int32, (picks, picks), 1
    )
    for t in range(steps):
        line = picked[t : t + 1, :]
        target_block = line // block_len
        source = jnp.zeros_like(line)
        for b in range(blocks):
            source = jnp.where(target_block == b, order[t, b], source)
        code = (source * block_len + line % block_len).astype(F32)
        column = jnp.sum(
            jnp.where(eye, jnp.broadcast_to(code, (picks, picks)), 0.0), axis=1, keepdims=True
        ).astype(jnp.int32)
        srcs[t * picks : (t + 1) * picks, :] = jnp.broadcast_to(column // block_len, (picks, 128))
        within = column % block_len
        low = parity_sign(within & lax.broadcasted_iota(jnp.int32, (picks, 128), 1)).astype(BF16)
        high = jnp.broadcast_to(within // 128, (picks, 128))
        for h in range(block_len // 128):
            walsh[t * picks : (t + 1) * picks, h * 128 : (h + 1) * 128] = low * parity_sign(
                high & h
            ).astype(BF16)
    small[2].wait()
    width = 2 * block_len
    acc[...] = jnp.zeros_like(acc)

    def build(pair, lhs):
        for b in range(2):
            here = pl.ds(pl.multiple_of(pair * width, width) + b * block_len, block_len)
            for t in range(steps):
                own = slice(t * picks, (t + 1) * picks)
                sign = (2 * fv[t : t + 1, here] - 1).astype(F32).astype(BF16)
                chosen = jnp.where(srcs[own, :] == 2 * pair + b, 1.0, 0.0).astype(BF16)
                for h in range(block_len // 128):
                    part = slice(h * 128, (h + 1) * 128)
                    place = slice(b * block_len + h * 128, b * block_len + (h + 1) * 128)
                    lhs[own, place] = walsh[own, part] * chosen * sign[:, part]

    def apply(pair, lhs):
        lanes = pl.ds(pl.multiple_of(pair * width, width), width)
        acc[...] += lax.dot_general(lhs[...], dv[:, lanes], NT, preferred_element_type=F32)

    def arrived(pair):
        for b in range(2):
            here = pl.ds(pl.multiple_of(pair * width, width) + b * block_len, block_len)
            pltpu.make_async_copy(
                design_ref.at[:, here], dv.at[:, here], in_sems.at[2 * pair + b]
            ).wait()

    build(0, lhs_a)

    @pl.loop(0, blocks // 4)
    def _(quad):
        arrived(2 * quad)
        arrived(2 * quad + 1)
        build(2 * quad + 1, lhs_b)
        apply(2 * quad, lhs_a)
        build(jnp.minimum(2 * quad + 2, blocks // 2 - 1), lhs_a)
        apply(2 * quad + 1, lhs_b)

    for half in range(2):
        lanes = slice(half * 128, (half + 1) * 128)
        for rb in range(16):
            for t in range(steps):
                first = t * picks + rb * 8
                tile = (acc[first : first + 8, lanes] * inv_root).astype(BF16)
                xs[2 * (half * 16 + rb) + t] = tile.astype(F32) * keep_scale

    pl.semaphore_wait(barrier, 63 + 6)

    def remote(src, dst, stage, peer):
        return pltpu.make_async_remote_copy(
            src_ref=src,
            dst_ref=dst,
            send_sem=send_sems.at[stage],
            recv_sem=recv_sems.at[stage],
            device_id=peer,
            device_id_type=MESH,
        )

    def hops(mask):
        ring = (0, 1, 2, 1)
        return (mask >> 5) + ring[mask >> 3 & 3] + ring[mask >> 1 & 3]

    def scatter(src, dst, stage):
        for mask in sorted(range(1, 64), key=lambda m: (-hops(m), m)):
            peer = row ^ mask
            remote(src.at[peer], dst.at[mask - 1], stage, (peer, col)).start()

    plane = sorted(range(1, 16), key=lambda m: (-hops(2 * m), m))

    def gather_z(full, stage):
        for k in (4, 3, 5, 2, 6, 1, 7):
            place = full.at[z, xy]
            remote(place, place, stage, z_peer(k)).start()

    def gather_xy(full, stage):
        for mask in plane:
            place = full.at[:, xy]
            peer = row ^ (2 * mask)
            remote(place, place, stage, (peer, col)).start()

    def all_of(buffer, stage):
        return remote(buffer, buffer, stage, (row, col))

    def total(own, parts):
        lines = [own] + [parts[lead] for lead in range(3)]
        for index in range(3, 63):
            lines[index % 4] = lines[index % 4] + parts[index]
        return (lines[0] + lines[1]) + (lines[2] + lines[3])

    scatter(xs, rs_s, 0)

    small[3].wait()
    acc_e[...] = jnp.zeros_like(acc_e)

    @pl.loop(0, blocks // 4)
    def _(part):
        lanes = pl.ds(pl.multiple_of(part * 2 * width, 2 * width), 2 * width)
        own = dv[pl.ds(pl.multiple_of(col * 64, 64), 64), lanes]
        both = jnp.concatenate([own, tv[:, lanes]], axis=0)
        acc_e[...] += lax.dot_general(both, dv[:, lanes], NT, preferred_element_type=F32)

    for half in range(2):
        lanes = slice(half * 128, (half + 1) * 128)
        for rb in range(16):
            xe[2 * (half * 16 + rb) + 1] = acc_e[rb * 4 : rb * 4 + 4, lanes]
            if rb < 8:
                xe[2 * (half * 16 + rb)] = acc_e[64 + rb * 4 : 68 + rb * 4, lanes]
            else:
                xe[2 * (half * 16 + rb)] = jnp.zeros((4, 128), F32)
    scatter(xe, rs_e, 1)
    all_of(rs_s, 0).wait_recv()
    sf[z, xy] = total(xs[row], rs_s)
    for k in (4, 3, 5, 2, 6, 1, 7):
        place = sf.at[z, xy]
        remote(place, place, 7 + k, z_peer(k)).start()

    def along_z(k):
        place = sf.at[(z + 8 - k) % 8, xy]
        if k:
            remote(place, place, 7 + k, z_peer(k)).wait_recv()

    def over_plane(k, stage):
        place = sf.at[(z + 8 - k) % 8, xy]
        for mask in plane:
            remote(place, place, stage, (row ^ (2 * mask), col)).start()

    even, odd = (0, 2, 6, 4), (1, 7, 3, 5)
    for parity, first, second in ((0, even, odd), (1, odd, even)):

        @pl.when(z_lo == parity)
        def _():
            for k in first:
                along_z(k)
                over_plane(k, 4)
            for k in second:
                along_z(k)

    sums[xy] = jnp.sum(
        tree([sf[i, xy] * sf[i, xy] for i in range(8)]), axis=0, keepdims=True
    )
    for mask in plane:
        remote(sums.at[xy], sums.at[xy], 17, (row ^ (2 * mask), col)).start()
    def send_rest(whose):
        for parity, second in ((0, odd), (1, even)):

            @pl.when((z_lo == parity) & (core == whose))
            def _():
                for k in second:
                    over_plane(k, 16)

    send_rest(0)
    all_of(rs_e, 1).wait_recv()
    ef[z, xy] = total(xe[row], rs_e)
    gather_z(ef, 3)
    all_of(sf.at[0:4, 0:15], 4).wait_recv()
    all_of(sums.at[0:15], 17).wait_recv()
    send_rest(1)

    def half_of(half):
        return jnp.concatenate([sf[2 * c + half].reshape(picks, 128) for c in range(4)], axis=0)

    shift = jnp.sum(tree([sums[i] for i in range(16)])) / unknowns
    unscale = 1.0 / shift
    unit = jnp.where(eye, 1.0, 0.0)
    first_half = half_of(0)
    top[...] = product(first_half, first_half, TN) * unscale + unit

    def after_top(done):
        if done == 1:
            all_of(rs_e.at[0:7], 3).wait_recv()
            gather_xy(ef, 5)
        if done == 6:
            all_of(sf.at[0:4, 0:15], 16).wait_recv()
            second_half = half_of(1)
            cross_ref[...] = product(half_of(0), second_half, TN) * unscale
            tail[...] = product(second_half, second_half, TN) * unscale + unit

    def after_low(done):
        if done == 5:
            all_of(ef.at[:, 0:15], 5).wait_recv()
            for half in range(2):
                lanes = slice(half * 128, (half + 1) * 128)
                for rb in range(8):
                    own_b[rb * 4 : rb * 4 + 4, lanes] = ef[2 * col + half, rb]

            @pl.when(core == 0)
            def _():
                bt[...] = own_b[...]
                remote(own_b, bt, 15, (row + 1, col)).start()

            @pl.when(core == 1)
            def _():
                for half in range(2):
                    lanes = slice(half * 128, (half + 1) * 128)
                    for c in range(4):
                        for rb in range(16):
                            first = c * 64 + rb * 4
                            gmat[first : first + 4, lanes] = ef[2 * c + half, rb]
                remote(gmat, gmat, 18, (row - 1, col)).start()

        if done == 6:
            lead = own_b[:, 0:128]
            lead_ref[...] = product(lead, top[...], NN)
            rest_ref[...] = own_b[:, 128:256] - product(lead, ratio_ref[...], NN)

    invert(top, after_top)
    ratio = product(top[...], cross_ref[...], NN)
    tail[...] = tail[...] - product(cross_ref[...], ratio, TN)
    ratio_ref[...] = ratio
    invert(tail, after_low)

    @pl.when(core == 0)
    def _():
        rest = product(rest_ref[...], tail[...], NN)
        lead = lead_ref[...] - product(rest, ratio_ref[...], NT)
        start_at[:, 0:128] = lead * unscale
        start_at[:, 128:256] = rest * unscale
        remote(start_at, start_at, 6, (row + 1, col)).start()
        remote(gmat, gmat, 18, (row + 1, col)).wait_recv()

    @pl.when(core == 1)
    def _():
        ratio = ratio_ref[...]
        corner = tail[...]
        across = product(ratio, corner, NN)
        last[0:128, 0:128] = (top[...] + product(across, ratio, NT)) * unscale
        last[0:128, 128:256] = across * -unscale
        last[128:256, 0:128] = product(corner, ratio, NT) * -unscale
        last[128:256, 128:256] = corner * unscale
        remote(last, last, 7, (row - 1, col)).start()
        remote(own_b, bt, 15, (row - 1, col)).wait_recv()
        remote(start_at, start_at, 6, (row - 1, col)).wait_recv()

    start = start_at[...]
    rounded = start.astype(BF16)
    gram_hi, gram_lo = split(gmat[...])
    gradient = jnp.dot(rounded, gram_hi, preferred_element_type=F32)
    gradient = gradient + jnp.dot(rounded, gram_lo, preferred_element_type=F32)
    gradient = gradient - bt[...]

    @pl.when(core == 0)
    def _():
        remote(last, last, 7, (row + 1, col)).wait_recv()

    out_ref[...] = start - product(gradient, last[...], NN)

    @pl.when(core == 0)
    def _():
        remote(start_at, start_at, 6, (row + 1, col)).wait_send()
        remote(own_b, bt, 15, (row + 1, col)).wait_send()

    @pl.when(core == 1)
    def _():
        remote(last, last, 7, (row - 1, col)).wait_send()
        remote(gmat, gmat, 18, (row - 1, col)).wait_send()

    all_of(rs_s, 0).wait_send()
    all_of(rs_e, 1).wait_send()
    for k in range(1, 8):
        remote(rs_s.at[0], rs_s.at[0], 7 + k, z_peer(k)).wait_send()
    all_of(rs_e.at[0:7], 3).wait_send()
    all_of(sf.at[0:4, 0:15], 4).wait_send()
    all_of(sf.at[0:4, 0:15], 16).wait_send()
    all_of(sums.at[0:15], 17).wait_send()
    all_of(ef.at[:, 0:15], 5).wait_send()


def residual_kernel(solved_ref, design_ref, targets_ref, solution_ref, residual_ref, parts, sems):
    pieces = parts.shape[0]
    width = parts.shape[2]
    rounded = solved_ref[...].astype(BF16)
    solution_copy = pltpu.make_async_copy(solved_ref, solution_ref, sems.at[pieces])
    solution_copy.start()
    copies = []
    for piece in range(pieces):
        lanes = slice(piece * width, (piece + 1) * width)
        product = jnp.dot(rounded, design_ref[:, lanes], preferred_element_type=F32)
        parts[piece] = product - targets_ref[:, lanes].astype(F32)
        copies.append(
            pltpu.make_async_copy(parts.at[piece], residual_ref.at[:, lanes], sems.at[piece])
        )
        copies[-1].start()
    for copy in copies:
        copy.wait()
    solution_copy.wait()


def on_device(design, targets, flip_bits, listed, block_order):
    unknowns, rows_here = design.shape
    block_len = rows_here // block_order.shape[2]
    rhs = targets.shape[0]
    order = block_order.reshape(2, block_order.shape[2])
    given = (order, design, targets, flip_bits, listed)
    solved, near_design, near_targets = pl.pallas_call(
        kernel,
        out_shape=(
            jax.ShapeDtypeStruct((rhs, unknowns), F32),
            jax.ShapeDtypeStruct(design.shape, BF16),
            jax.ShapeDtypeStruct(targets.shape, BF16),
        ),
        in_specs=[pl.BlockSpec(memory_space=pltpu.HBM)] * 5,
        out_specs=[pl.BlockSpec(memory_space=pltpu.VMEM)] * 3,
        scratch_shapes=[
            pltpu.SMEM((2, block_order.shape[2]), jnp.int32),
            pltpu.VMEM((2, rows_here), jnp.int32),
            pltpu.VMEM((2, 512), jnp.int32),
            pltpu.VMEM((256, block_len), BF16),
            pltpu.VMEM((256, 128), jnp.int32),
            pltpu.VMEM((256, 2 * block_len), BF16),
            pltpu.VMEM((256, 2 * block_len), BF16),
            pltpu.VMEM((256, unknowns), F32),
            pltpu.VMEM((96, unknowns), F32),
            pltpu.VMEM((64, 8, 128), F32),
            pltpu.VMEM((64, 4, 128), F32),
            pltpu.VMEM((63, 8, 128), F32),
            pltpu.VMEM((63, 4, 128), F32),
            pltpu.VMEM((8, 16, 8, 128), F32),
            pltpu.VMEM((8, 16, 4, 128), F32),
            pltpu.VMEM((128, 128), F32),
            pltpu.VMEM((rhs, unknowns), F32),
            pltpu.VMEM((rhs, 128), F32),
            pltpu.VMEM((rhs, 128), F32),
            pltpu.VMEM((unknowns, unknowns), F32),
            pltpu.VMEM((rhs, unknowns), F32),
            pltpu.VMEM((rhs, unknowns), F32),
            pltpu.VMEM((unknowns, unknowns), F32),
            pltpu.VMEM((128, 128), F32),
            pltpu.VMEM((128, 128), F32),
            pltpu.VMEM((128, 128), F32),
            pltpu.VMEM((16, 1, 128), F32),
            pltpu.SemaphoreType.DMA((block_order.shape[2] + 4,)),
            pltpu.SemaphoreType.DMA((19,)),
            pltpu.SemaphoreType.DMA((19,)),
        ],
        compiler_params=pltpu.CompilerParams(
            collective_id=0, has_side_effects=True, vmem_limit_bytes=40 * 1024 * 1024
        ),
        name="sketch_solve",
    )(*(pltpu.with_memory_space_constraint(v, pltpu.HBM) for v in given))
    out, residual = pl.pallas_call(
        residual_kernel,
        out_shape=(
            jax.ShapeDtypeStruct((rhs, unknowns), F32),
            jax.ShapeDtypeStruct(targets.shape, F32),
        ),
        in_specs=[pl.BlockSpec(memory_space=pltpu.VMEM)] * 3,
        out_specs=[pl.BlockSpec(memory_space=pltpu.HBM)] * 2,
        scratch_shapes=[
            pltpu.VMEM((8, rhs, rows_here // 8), F32),
            pltpu.SemaphoreType.DMA((9,)),
        ],
        compiler_params=pltpu.CompilerParams(vmem_limit_bytes=16 * 1024 * 1024),
        name="residual",
    )(solved, near_design, near_targets)
    return (out.T, residual)


def solution(mesh):
    return jax.shard_map(
        on_device,
        mesh=mesh,
        in_specs=(
            P(None, "rows"),
            P("cols", "rows"),
            P(None, "rows"),
            P(None, "rows"),
            P(None, "rows", None),
        ),
        out_specs=(P(None, "cols"), P("cols", "rows")),
        check_vma=False,
    )
```

```python
import functools
import math

import jax
import jax.numpy as jnp
from jax import lax
from jax.experimental import pallas as pl
from jax.experimental.pallas import tpu as pltpu
from jax.sharding import PartitionSpec as P

MESH = pl.DeviceIdType.MESH
F32 = jnp.float32
BF16 = jnp.bfloat16
NB = 16
NT = (((1,), (1,)), ((), ()))
TN = (((0,), (0,)), ((), ()))
NN = (((1,), (0,)), ((), ()))


def parity_sign(bits):
    bits = bits ^ (bits >> 4)
    bits = bits ^ (bits >> 2)
    bits = (bits ^ (bits >> 1)) & 1
    return (1 - 2 * bits).astype(F32)


def product(a, b, dims):
    (a_hi, a_lo), (b_hi, b_lo) = split(a), split(b)
    out = lax.dot_general(a_hi, b_hi, dims, preferred_element_type=F32)
    out = out + lax.dot_general(a_hi, b_lo, dims, preferred_element_type=F32)
    return out + lax.dot_general(a_lo, b_hi, dims, preferred_element_type=F32)


def split(x):
    hi = x.astype(BF16)
    return hi, (x - hi.astype(F32)).astype(BF16)


def lane_of(tile, c):
    return jnp.broadcast_to(tile[:, c : c + 1], (8, 128))


def row_of(tile, j):
    return jnp.broadcast_to(tile[j : j + 1, :], (8, 128))


def tree(terms):
    while len(terms) > 1:
        paired = [terms[i] + terms[i + 1] for i in range(0, len(terms) - 1, 2)]
        terms = paired + ([terms[-1]] if len(terms) % 2 else [])
    return terms[0]


def small_inverse(cols, sub):
    for q in range(0, 8, 2):
        a, b, c = row_of(cols[q], q), row_of(cols[q + 1], q), row_of(cols[q + 1], q + 1)
        r = 1.0 / (a * c - b * b)
        t0, t1 = cols[q] * c - cols[q + 1] * b, cols[q + 1] * a - cols[q] * b
        t0 = jnp.where(sub == q, -c, jnp.where(sub == q + 1, b, t0))
        t1 = jnp.where(sub == q, b, jnp.where(sub == q + 1, -a, t1))
        fresh = []
        for j in range(8):
            if j == q:
                fresh.append(-(r * t0))
            elif j == q + 1:
                fresh.append(-(r * t1))
            else:
                kept = jnp.where((sub == q) | (sub == q + 1), 0.0, cols[j])
                fresh.append(kept - r * (t0 * row_of(cols[j], q) + t1 * row_of(cols[j], q + 1)))
        cols = fresh
    return cols


def eliminate(tiles, k0, sub, lane):
    home = k0 // 128
    groups = NB // 8
    ahead = None
    for s in range(groups):
        c0 = k0 + 8 * s - 128 * home
        diagonal = ahead or [lane_of(tiles[s][home], c0 + j) for j in range(8)]
        inverse = small_inverse(diagonal, sub)
        if s + 1 < groups:
            low = [lane_of(tiles[s + 1][home], c0 + j) for j in range(8)]
            after = [lane_of(tiles[s + 1][home], c0 + 8 + j) for j in range(8)]
            scaled = [
                tree([low[i] * row_of(inverse[j], i) for i in range(8)]) for j in range(8)
            ]
            ahead = [
                after[j] - tree([scaled[i] * row_of(low[i], j) for i in range(8)])
                for j in range(8)
            ]
        cols = [
            [diagonal[j] if g == s else lane_of(tiles[g][home], c0 + j) for g in range(groups)]
            for j in range(8)
        ]
        inside = (lane >= c0) & (lane < c0 + 8)
        unit = jnp.where(lane == sub + c0, 1.0, 0.0)
        lead = [jnp.where(inside, unit, t) if h == home else t for h, t in enumerate(tiles[s])]
        fresh = [tree([inverse[j] * row_of(t, j) for j in range(8)]) for t in lead]
        rows = [[row_of(t, j) for j in range(8)] for t in fresh]
        moved = [None] * groups
        moved[s] = fresh
        for g in [(s + d) % groups for d in range(1, groups)]:
            line = []
            for h, tile in enumerate(tiles[g]):
                kept = jnp.where(inside, 0.0, tile) if h == home else tile
                line.append(kept - tree([cols[j][g] * rows[h][j] for j in range(8)]))
            moved[g] = line
        tiles = moved
    return tiles


def invert(mat, after_round):
    n = mat.shape[0]
    sub = lax.broadcasted_iota(jnp.int32, (8, 128), 0)
    lane = lax.broadcasted_iota(jnp.int32, (8, 128), 1)
    wide = lax.broadcasted_iota(jnp.int32, (NB, n), 1)
    panel = mat[0:NB, :]
    for k0 in range(0, n, NB):
        k1 = k0 + NB
        left_hi, left_lo = split(jnp.where(wide < k0, -panel, panel))
        left = jnp.concatenate([left_hi, left_hi, left_lo], axis=0)
        tiles = [
            [panel[8 * g : 8 * g + 8, lane0 : lane0 + 128] for lane0 in range(0, n, 128)]
            for g in range(NB // 8)
        ]
        tiles = eliminate(tiles, k0, sub, lane)
        done = jnp.concatenate([jnp.concatenate(t, axis=1) for t in tiles], axis=0)
        right_hi, right_lo = split(done)
        right = jnp.concatenate([right_hi, right_lo, right_hi], axis=0)
        inside = (wide >= k0) & (wide < k1)
        if k1 < n:
            first = lax.dot_general(left[:, k1 : k1 + NB], right, TN, preferred_element_type=F32)
            panel = jnp.where(inside, 0.0, mat[k1 : k1 + NB, :]) - first
        update = lax.dot_general(left, right, TN, preferred_element_type=F32)
        for other in range(0, n, NB):
            here = slice(other, other + NB)
            if other == k0:
                mat[here, :] = done
            elif other != k1:
                mat[here, :] = jnp.where(inside, 0.0, mat[here, :]) - update[here, :]
        after_round(k0 // NB)


def kernel(
    order_ref,
    design_ref,
    targets_ref,
    flips_ref,
    listed_ref,
    out_ref,
    dv,
    tv,
    order,
    fv,
    lv,
    walsh,
    srcs,
    lhs_a,
    lhs_b,
    acc,
    acc_e,
    xs,
    xe,
    rs_s,
    rs_e,
    sf,
    ef,
    cross_ref,
    own_b,
    lead_ref,
    rest_ref,
    gmat,
    bt,
    start_at,
    last,
    top,
    tail,
    ratio_ref,
    sums,
    in_sems,
    send_sems,
    recv_sems,
):
    unknowns = dv.shape[0]
    rows_here = dv.shape[1]
    block_len = walsh.shape[1]
    blocks = rows_here // block_len
    steps = 2
    picks = 128
    inv_root = 1.0 / math.sqrt(block_len)
    keep_scale = math.sqrt(rows_here / listed_ref.shape[1])
    row = lax.axis_index("rows")
    col = lax.axis_index("cols")
    core = row % 2
    xy = (row // 2) % 16
    z_lo = row // 32
    z = col * 2 + z_lo

    def chunk_copy(b):
        lanes = pl.ds(b * block_len, block_len)
        return pltpu.make_async_copy(design_ref.at[:, lanes], dv.at[:, lanes], in_sems.at[b])

    small = (
        pltpu.make_async_copy(order_ref, order, in_sems.at[blocks + 3]),
        pltpu.make_async_copy(listed_ref, lv, in_sems.at[blocks]),
        pltpu.make_async_copy(flips_ref, fv, in_sems.at[blocks + 1]),
        pltpu.make_async_copy(targets_ref, tv, in_sems.at[blocks + 2]),
    )
    small[0].start()
    small[1].start()
    small[2].start()
    chunk_copy(0).start()
    small[3].start()
    for b in range(1, blocks):
        chunk_copy(b).start()

    barrier = pltpu.get_barrier_semaphore()

    def z_peer(k):
        other = (z + k) % 8
        return ((other % 2) * 32 + row % 32, other // 2)

    for mask in range(1, 64):
        pl.semaphore_signal(barrier, inc=1, device_id=(row ^ mask, col), device_id_type=MESH)

    for mask in range(2, 8):
        other = z ^ mask
        peer = ((other % 2) * 32 + row % 32, other // 2)
        pl.semaphore_signal(barrier, inc=1, device_id=peer, device_id_type=MESH)

    small[0].wait()
    small[1].wait()
    picked = lv[:, pl.ds(pl.multiple_of(col * picks, picks), picks)]
    eye = lax.broadcasted_iota(jnp.int32, (picks, picks), 0) == lax.broadcasted_iota(
        jnp.int32, (picks, picks), 1
    )
    for t in range(steps):
        line = picked[t : t + 1, :]
        target_block = line // block_len
        source = jnp.zeros_like(line)
        for b in range(blocks):
            source = jnp.where(target_block == b, order[t, b], source)
        code = (source * block_len + line % block_len).astype(F32)
        column = jnp.sum(
            jnp.where(eye, jnp.broadcast_to(code, (picks, picks)), 0.0), axis=1, keepdims=True
        ).astype(jnp.int32)
        srcs[t * picks : (t + 1) * picks, :] = jnp.broadcast_to(column // block_len, (picks, 128))
        within = column % block_len
        low = parity_sign(within & lax.broadcasted_iota(jnp.int32, (picks, 128), 1)).astype(BF16)
        high = jnp.broadcast_to(within // 128, (picks, 128))
        for h in range(block_len // 128):
            walsh[t * picks : (t + 1) * picks, h * 128 : (h + 1) * 128] = low * parity_sign(
                high & h
            ).astype(BF16)
    small[2].wait()
    width = 2 * block_len
    acc[...] = jnp.zeros_like(acc)

    def build(pair, lhs):
        for b in range(2):
            here = pl.ds(pl.multiple_of(pair * width, width) + b * block_len, block_len)
            for t in range(steps):
                own = slice(t * picks, (t + 1) * picks)
                sign = (2 * fv[t : t + 1, here] - 1).astype(F32).astype(BF16)
                chosen = jnp.where(srcs[own, :] == 2 * pair + b, 1.0, 0.0).astype(BF16)
                for h in range(block_len // 128):
                    part = slice(h * 128, (h + 1) * 128)
                    place = slice(b * block_len + h * 128, b * block_len + (h + 1) * 128)
                    lhs[own, place] = walsh[own, part] * chosen * sign[:, part]

    def apply(pair, lhs):
        lanes = pl.ds(pl.multiple_of(pair * width, width), width)
        acc[...] += lax.dot_general(lhs[...], dv[:, lanes], NT, preferred_element_type=F32)

    def arrived(pair):
        for b in range(2):
            here = pl.ds(pl.multiple_of(pair * width, width) + b * block_len, block_len)
            pltpu.make_async_copy(
                design_ref.at[:, here], dv.at[:, here], in_sems.at[2 * pair + b]
            ).wait()

    build(0, lhs_a)

    @pl.loop(0, blocks // 4)
    def _(quad):
        arrived(2 * quad)
        arrived(2 * quad + 1)
        build(2 * quad + 1, lhs_b)
        apply(2 * quad, lhs_a)
        build(jnp.minimum(2 * quad + 2, blocks // 2 - 1), lhs_a)
        apply(2 * quad + 1, lhs_b)

    for half in range(2):
        lanes = slice(half * 128, (half + 1) * 128)
        for rb in range(16):
            for t in range(steps):
                first = t * picks + rb * 8
                tile = (acc[first : first + 8, lanes] * inv_root).astype(BF16)
                xs[2 * (half * 16 + rb) + t] = tile.astype(F32) * keep_scale

    pl.semaphore_wait(barrier, 63 + 6)

    def remote(src, dst, stage, peer):
        return pltpu.make_async_remote_copy(
            src_ref=src,
            dst_ref=dst,
            send_sem=send_sems.at[stage],
            recv_sem=recv_sems.at[stage],
            device_id=peer,
            device_id_type=MESH,
        )

    def hops(mask):
        ring = (0, 1, 2, 1)
        return (mask >> 5) + ring[mask >> 3 & 3] + ring[mask >> 1 & 3]

    def scatter(src, dst, stage):
        for mask in sorted(range(1, 64), key=lambda m: (-hops(m), m)):
            peer = row ^ mask
            remote(src.at[peer], dst.at[mask - 1], stage, (peer, col)).start()

    plane = sorted(range(1, 16), key=lambda m: (-hops(2 * m), m))

    def gather_z(full, stage):
        for k in (4, 3, 5, 2, 6, 1, 7):
            place = full.at[z, xy]
            remote(place, place, stage, z_peer(k)).start()

    def gather_xy(full, stage):
        for mask in plane:
            place = full.at[:, xy]
            peer = row ^ (2 * mask)
            remote(place, place, stage, (peer, col)).start()

    def all_of(buffer, stage):
        return remote(buffer, buffer, stage, (row, col))

    def total(own, parts):
        lines = [own] + [parts[lead] for lead in range(3)]
        for index in range(3, 63):
            lines[index % 4] = lines[index % 4] + parts[index]
        return (lines[0] + lines[1]) + (lines[2] + lines[3])

    scatter(xs, rs_s, 0)

    small[3].wait()
    acc_e[...] = jnp.zeros_like(acc_e)

    @pl.loop(0, blocks // 4)
    def _(part):
        lanes = pl.ds(pl.multiple_of(part * 2 * width, 2 * width), 2 * width)
        own = dv[pl.ds(pl.multiple_of(col * 64, 64), 64), lanes]
        both = jnp.concatenate([own, tv[:, lanes]], axis=0)
        acc_e[...] += lax.dot_general(both, dv[:, lanes], NT, preferred_element_type=F32)

    for half in range(2):
        lanes = slice(half * 128, (half + 1) * 128)
        for rb in range(16):
            xe[2 * (half * 16 + rb) + 1] = acc_e[rb * 4 : rb * 4 + 4, lanes]
            if rb < 8:
                xe[2 * (half * 16 + rb)] = acc_e[64 + rb * 4 : 68 + rb * 4, lanes]
            else:
                xe[2 * (half * 16 + rb)] = jnp.zeros((4, 128), F32)
    scatter(xe, rs_e, 1)
    all_of(rs_s, 0).wait_recv()
    sf[z, xy] = total(xs[row], rs_s)
    for k in (4, 3, 5, 2, 6, 1, 7):
        place = sf.at[z, xy]
        remote(place, place, 7 + k, z_peer(k)).start()

    def along_z(k):
        place = sf.at[(z + 8 - k) % 8, xy]
        if k:
            remote(place, place, 7 + k, z_peer(k)).wait_recv()

    def over_plane(k, stage):
        place = sf.at[(z + 8 - k) % 8, xy]
        for mask in plane:
            remote(place, place, stage, (row ^ (2 * mask), col)).start()

    even, odd = (0, 2, 6, 4), (1, 7, 3, 5)
    for parity, first, second in ((0, even, odd), (1, odd, even)):

        @pl.when(z_lo == parity)
        def _():
            for k in first:
                along_z(k)
                over_plane(k, 4)
            for k in second:
                along_z(k)

    sums[xy] = jnp.sum(
        tree([sf[i, xy] * sf[i, xy] for i in range(8)]), axis=0, keepdims=True
    )
    for mask in plane:
        remote(sums.at[xy], sums.at[xy], 17, (row ^ (2 * mask), col)).start()
    def send_rest(whose, tiles):
        for parity, second in ((0, odd), (1, even)):

            @pl.when((z_lo == parity) & (core == whose))
            def _():
                for k in second[tiles]:
                    over_plane(k, 16)

    send_rest(0, slice(0, 4))
    send_rest(1, slice(0, 1))
    all_of(rs_e, 1).wait_recv()
    ef[z, xy] = total(xe[row], rs_e)
    gather_z(ef, 3)
    all_of(sf.at[0:4, 0:15], 4).wait_recv()
    all_of(sums.at[0:15], 17).wait_recv()
    send_rest(1, slice(1, 4))

    def half_of(half):
        return jnp.concatenate([sf[2 * c + half].reshape(picks, 128) for c in range(4)], axis=0)

    shift = jnp.sum(tree([sums[i] for i in range(16)])) / unknowns
    unscale = 1.0 / shift
    unit = jnp.where(eye, 1.0, 0.0)
    first_half = half_of(0)
    top[...] = product(first_half, first_half, TN) * unscale + unit

    def after_top(done):
        if done == 1:
            all_of(rs_e.at[0:7], 3).wait_recv()
            gather_xy(ef, 5)
        if done == 6:
            all_of(sf.at[0:4, 0:15], 16).wait_recv()
            second_half = half_of(1)
            cross_ref[...] = product(half_of(0), second_half, TN) * unscale
            tail[...] = product(second_half, second_half, TN) * unscale + unit

    def after_low(done):
        if done == 5:
            all_of(ef.at[:, 0:15], 5).wait_recv()
            for half in range(2):
                lanes = slice(half * 128, (half + 1) * 128)
                for rb in range(8):
                    own_b[rb * 4 : rb * 4 + 4, lanes] = ef[2 * col + half, rb]

            @pl.when(core == 0)
            def _():
                bt[...] = own_b[...]
                remote(own_b, bt, 15, (row + 1, col)).start()

            @pl.when(core == 1)
            def _():
                for half in range(2):
                    lanes = slice(half * 128, (half + 1) * 128)
                    for c in range(4):
                        for rb in range(16):
                            first = c * 64 + rb * 4
                            gmat[first : first + 4, lanes] = ef[2 * c + half, rb]
                remote(gmat, gmat, 18, (row - 1, col)).start()

        if done == 6:
            lead = own_b[:, 0:128]
            lead_ref[...] = product(lead, top[...], NN)
            rest_ref[...] = own_b[:, 128:256] - product(lead, ratio_ref[...], NN)

    invert(top, after_top)
    ratio = product(top[...], cross_ref[...], NN)
    tail[...] = tail[...] - product(cross_ref[...], ratio, TN)
    ratio_ref[...] = ratio
    invert(tail, after_low)

    @pl.when(core == 0)
    def _():
        rest = product(rest_ref[...], tail[...], NN)
        lead = lead_ref[...] - product(rest, ratio_ref[...], NT)
        start_at[:, 0:128] = lead * unscale
        start_at[:, 128:256] = rest * unscale
        remote(start_at, start_at, 6, (row + 1, col)).start()
        remote(gmat, gmat, 18, (row + 1, col)).wait_recv()

    @pl.when(core == 1)
    def _():
        ratio = ratio_ref[...]
        corner = tail[...]
        across = product(ratio, corner, NN)
        last[0:128, 0:128] = (top[...] + product(across, ratio, NT)) * unscale
        last[0:128, 128:256] = across * -unscale
        last[128:256, 0:128] = product(corner, ratio, NT) * -unscale
        last[128:256, 128:256] = corner * unscale
        remote(last, last, 7, (row - 1, col)).start()
        remote(own_b, bt, 15, (row - 1, col)).wait_recv()
        remote(start_at, start_at, 6, (row - 1, col)).wait_recv()

    start = start_at[...]
    rounded = start.astype(BF16)
    gram_hi, gram_lo = split(gmat[...])
    gradient = jnp.dot(rounded, gram_hi, preferred_element_type=F32)
    gradient = gradient + jnp.dot(rounded, gram_lo, preferred_element_type=F32)
    gradient = gradient - bt[...]

    @pl.when(core == 0)
    def _():
        remote(last, last, 7, (row + 1, col)).wait_recv()

    out_ref[...] = start - product(gradient, last[...], NN)

    @pl.when(core == 0)
    def _():
        remote(start_at, start_at, 6, (row + 1, col)).wait_send()
        remote(own_b, bt, 15, (row + 1, col)).wait_send()

    @pl.when(core == 1)
    def _():
        remote(last, last, 7, (row - 1, col)).wait_send()
        remote(gmat, gmat, 18, (row - 1, col)).wait_send()

    all_of(rs_s, 0).wait_send()
    all_of(rs_e, 1).wait_send()
    for k in range(1, 8):
        remote(rs_s.at[0], rs_s.at[0], 7 + k, z_peer(k)).wait_send()
    all_of(rs_e.at[0:7], 3).wait_send()
    all_of(sf.at[0:4, 0:15], 4).wait_send()
    all_of(sf.at[0:4, 0:15], 16).wait_send()
    all_of(sums.at[0:15], 17).wait_send()
    all_of(ef.at[:, 0:15], 5).wait_send()


def residual_kernel(solved_ref, design_ref, targets_ref, solution_ref, residual_ref, parts, sems):
    pieces = parts.shape[0]
    width = parts.shape[2]
    rounded = solved_ref[...].astype(BF16)
    solution_copy = pltpu.make_async_copy(solved_ref, solution_ref, sems.at[pieces])
    solution_copy.start()
    copies = []
    for piece in range(pieces):
        lanes = slice(piece * width, (piece + 1) * width)
        product = jnp.dot(rounded, design_ref[:, lanes], preferred_element_type=F32)
        parts[piece] = product - targets_ref[:, lanes].astype(F32)
        copies.append(
            pltpu.make_async_copy(parts.at[piece], residual_ref.at[:, lanes], sems.at[piece])
        )
        copies[-1].start()
    for copy in copies:
        copy.wait()
    solution_copy.wait()


def on_device(design, targets, flip_bits, listed, block_order):
    unknowns, rows_here = design.shape
    block_len = rows_here // block_order.shape[2]
    rhs = targets.shape[0]
    order = block_order.reshape(2, block_order.shape[2])
    given = (order, design, targets, flip_bits, listed)
    solved, near_design, near_targets = pl.pallas_call(
        kernel,
        out_shape=(
            jax.ShapeDtypeStruct((rhs, unknowns), F32),
            jax.ShapeDtypeStruct(design.shape, BF16),
            jax.ShapeDtypeStruct(targets.shape, BF16),
        ),
        in_specs=[pl.BlockSpec(memory_space=pltpu.HBM)] * 5,
        out_specs=[pl.BlockSpec(memory_space=pltpu.VMEM)] * 3,
        scratch_shapes=[
            pltpu.SMEM((2, block_order.shape[2]), jnp.int32),
            pltpu.VMEM((2, rows_here), jnp.int32),
            pltpu.VMEM((2, 512), jnp.int32),
            pltpu.VMEM((256, block_len), BF16),
            pltpu.VMEM((256, 128), jnp.int32),
            pltpu.VMEM((256, 2 * block_len), BF16),
            pltpu.VMEM((256, 2 * block_len), BF16),
            pltpu.VMEM((256, unknowns), F32),
            pltpu.VMEM((96, unknowns), F32),
            pltpu.VMEM((64, 8, 128), F32),
            pltpu.VMEM((64, 4, 128), F32),
            pltpu.VMEM((63, 8, 128), F32),
            pltpu.VMEM((63, 4, 128), F32),
            pltpu.VMEM((8, 16, 8, 128), F32),
            pltpu.VMEM((8, 16, 4, 128), F32),
            pltpu.VMEM((128, 128), F32),
            pltpu.VMEM((rhs, unknowns), F32),
            pltpu.VMEM((rhs, 128), F32),
            pltpu.VMEM((rhs, 128), F32),
            pltpu.VMEM((unknowns, unknowns), F32),
            pltpu.VMEM((rhs, unknowns), F32),
            pltpu.VMEM((rhs, unknowns), F32),
            pltpu.VMEM((unknowns, unknowns), F32),
            pltpu.VMEM((128, 128), F32),
            pltpu.VMEM((128, 128), F32),
            pltpu.VMEM((128, 128), F32),
            pltpu.VMEM((16, 1, 128), F32),
            pltpu.SemaphoreType.DMA((block_order.shape[2] + 4,)),
            pltpu.SemaphoreType.DMA((19,)),
            pltpu.SemaphoreType.DMA((19,)),
        ],
        compiler_params=pltpu.CompilerParams(
            collective_id=0, has_side_effects=True, vmem_limit_bytes=40 * 1024 * 1024
        ),
        name="sketch_solve",
    )(*(pltpu.with_memory_space_constraint(v, pltpu.HBM) for v in given))
    out, residual = pl.pallas_call(
        residual_kernel,
        out_shape=(
            jax.ShapeDtypeStruct((rhs, unknowns), F32),
            jax.ShapeDtypeStruct(targets.shape, F32),
        ),
        in_specs=[pl.BlockSpec(memory_space=pltpu.VMEM)] * 3,
        out_specs=[pl.BlockSpec(memory_space=pltpu.HBM)] * 2,
        scratch_shapes=[
            pltpu.VMEM((8, rhs, rows_here // 8), F32),
            pltpu.SemaphoreType.DMA((9,)),
        ],
        compiler_params=pltpu.CompilerParams(vmem_limit_bytes=16 * 1024 * 1024),
        name="residual",
    )(solved, near_design, near_targets)
    return (out.T, residual)


def solution(mesh):
    return jax.shard_map(
        on_device,
        mesh=mesh,
        in_specs=(
            P(None, "rows"),
            P("cols", "rows"),
            P(None, "rows"),
            P(None, "rows"),
            P(None, "rows", None),
        ),
        out_specs=(P(None, "cols"), P("cols", "rows")),
        check_vma=False,
    )
```
